1024 devices in a mesh: row: 64 (over z, x), col: 16 (over y, core).
Axes of the slice: x: 4, y: 8, z: 16, core: 2. Of those that a mesh axis runs over, the one named last changes fastest.
Arguments:
- upper_tiles: float32 [1024, 3, 256, 256], P(('row', 'col')), as said below
- listed_mask: int32 [1024, 3], P(('row', 'col')), may hold values from 0 to 1, as said below
Outputs:
- purified: float32 [1024, 3, 256, 256], P(('row', 'col'))
- square_traces: float32 [2], replicated
The draws below stay inside these ranges and needn't reach their ends.
Inputs may be any that keep to these rules, and one draw needn't show every extreme that they name: `upper_tiles`: slot 0 of every tile row holds a symmetric tile. `listed_mask`: slot 0 of every tile row is listed.
All inputs are finite; a program needn't handle non-finite values.
Results may differ from the reference program's by a relative error of at most 0.0003.
Values sent between devices are 32-bit elements; how exact they have to be, the bound alone decides.
No kernel may reach another device: no remote copies, remote signals or barrier semaphores. Data moves between devices by JAX's collectives and lax.ppermute only.
A program may use at most 32 MiB of HBM per device.

```python
import jax
import jax.numpy as jnp
from jax import lax

TILE = 256
BAND = 3
STEPS = 2
TILE_ROWS = 1024


def draw_upper_tiles(key, part):
    first, second = jax.random.split(key, 2)
    shape = (TILE_ROWS, BAND, TILE, TILE)
    noise = jax.random.normal(first, shape, jnp.float32)
    noise = 0.01 * noise
    diag_noise = noise[:, 0]
    symmetric = 0.5 * (diag_noise + jnp.swapaxes(diag_noise, 1, 2))
    fraction = jnp.arange(TILE_ROWS, dtype=jnp.float32) / max(TILE_ROWS - 1, 1)
    shifted = 0.3 + 0.4 * fraction + 0.05 * jax.random.uniform(second, (TILE_ROWS,), jnp.float32)
    identity = jnp.eye(TILE, dtype=jnp.float32)
    diag_tile = symmetric + shifted[:, None, None] * identity[None, :, :]
    return noise.at[:, 0].set(diag_tile)


def draw_listed_mask(key, part):
    first, second = jax.random.split(key, 2)
    levels = jax.random.randint(first, (TILE_ROWS, 1), 0, BAND)
    picks = jax.random.randint(second, (TILE_ROWS, BAND), 0, BAND - 1)
    listed = (picks < levels).astype(jnp.int32)
    slots = jnp.arange(BAND, dtype=jnp.int32)
    return jnp.where(slots[None, :] == 0, 1, listed).astype(jnp.int32)


def setup_inputs(seed: int = 0) -> dict:
    key_of = jax.random.split(jax.random.key(seed), 3)
    upper_tiles = draw_upper_tiles(jax.random.fold_in(key_of[2], 71), 0)
    listed_mask = draw_listed_mask(jax.random.fold_in(key_of[2], 71), 0)
    return {"upper_tiles": upper_tiles, "listed_mask": listed_mask}


def tile_of(window, span, position, target):
    if target < position:
        return jnp.transpose(tile_of(window, span, target, position))
    return window[position + span][target - position]


def reference(upper_tiles, listed_mask):
    span = BAND - 1
    slots = jnp.arange(BAND, dtype=jnp.int32)
    row_ids = jnp.arange(TILE_ROWS, dtype=jnp.int32)
    inside = (row_ids[:, None] + slots[None, :] < TILE_ROWS).astype(jnp.int32)
    listed = listed_mask * inside
    weights = listed.astype(jnp.float32)[:, :, None, None]
    current = upper_tiles * weights
    traces = []
    for step in range(STEPS):
        padded = jnp.pad(current, ((span, span), (0, 0), (0, 0), (0, 0)))

        def one_row(row_index):
            window = lax.dynamic_slice_in_dim(padded, row_index.astype(jnp.int32), 2 * span + 1, 0)
            results = []
            for offset in range(BAND):
                total = jnp.zeros((TILE, TILE), jnp.float32)
                for middle in range(offset - span, span + 1):
                    left_tile = tile_of(window, span, 0, middle)
                    right_tile = tile_of(window, span, middle, offset)
                    total = total + jnp.dot(left_tile, right_tile, precision=lax.Precision.HIGHEST, preferred_element_type=jnp.float32)
                results.append(total)
            return jnp.stack(results)

        square = lax.map(one_row, row_ids)
        traces.append(jnp.sum(jnp.trace(square[:, 0], axis1=1, axis2=2)))
        if step % 2 == 0:
            current = (2.0 * current - square) * weights
        else:
            current = square * weights
    return current, jnp.stack(traces) / TILE
```

```python
import functools

import jax
import jax.numpy as jnp
from jax import lax
from jax.experimental import pallas as pl
from jax.experimental.pallas import tpu as pltpu
from jax.sharding import PartitionSpec as P

STEPS = 2
AXES = ("row", "col")
LANES = 128


def shift(value, steps):
    count = lax.axis_size(AXES)
    first, last = (max(0, -steps), min(count, count - steps))
    return lax.ppermute(value, AXES, [(source, source + steps) for source in range(first, last)])


def split(tile):
    high = tile.astype(jnp.bfloat16)
    return (high, (tile - high.astype(jnp.float32)).astype(jnp.bfloat16))


def product(left, right, left_dim, right_dim):
    def one(a, b):
        return lax.dot_general(
            a, b, (((left_dim,), (right_dim,)), ((), ())), preferred_element_type=jnp.float32
        )

    return one(left[0], right[0]) + (one(left[0], right[1]) + one(left[1], right[0]))


def squared_norm(tiles):
    total = tiles[0] * tiles[0] + 2.0 * (tiles[1] * tiles[1] + tiles[2] * tiles[2])
    return jnp.sum(total)


def step_kernel(even, weights, own, behind1, behind2, ahead1, ahead2, out, *norms):
    own_f = [own[slot] for slot in range(3)]
    c0, c1, c2 = (split(tile) for tile in own_f)
    b10, b11 = (split(behind1[0]), split(behind1[1]))
    b22 = split(behind2[0])
    a10, a11 = (split(ahead1[0]), split(ahead1[1]))
    a20 = split(ahead2[0])
    squares = (
        product(c0, c0, 1, 0)
        + product(c1, c1, 1, 1)
        + product(c2, c2, 1, 1)
        + product(b10, b10, 0, 0)
        + product(b22, b22, 0, 0),
        product(c0, c1, 1, 0)
        + product(c1, a10, 1, 0)
        + product(c2, a11, 1, 1)
        + product(b10, b11, 0, 0),
        product(c0, c2, 1, 0) + product(c1, a11, 1, 0) + product(c2, a20, 1, 0),
    )
    fresh = []
    for slot in range(3):
        value = 2.0 * own_f[slot] - squares[slot] if even else squares[slot]
        fresh.append(value * weights[slot])
        out[slot] = fresh[slot]
    if norms:
        (pay,) = norms
        lane = lax.broadcasted_iota(jnp.int32, pay.shape, 1)
        pay[...] = jnp.where(lane == 0, squared_norm(own_f), squared_norm(fresh))


def step(even, weights, own, behind1, behind2, ahead1, ahead2, pay_rows):
    vmem = pl.BlockSpec(memory_space=pltpu.VMEM)
    shapes = [jax.ShapeDtypeStruct(own.shape, jnp.float32)]
    if pay_rows:
        shapes.append(jax.ShapeDtypeStruct((pay_rows, LANES), jnp.float32))
    order = own.shape[-1]
    return pl.pallas_call(
        functools.partial(step_kernel, even),
        out_shape=shapes,
        in_specs=[pl.BlockSpec(memory_space=pltpu.SMEM)] + [vmem] * 5,
        out_specs=[vmem] * len(shapes),
        compiler_params=pltpu.CompilerParams(vmem_limit_bytes=24 * 1024 * 1024),
        cost_estimate=pl.CostEstimate(
            flops=36 * 2 * order**3, bytes_accessed=12 * 4 * order**2, transcendentals=0
        ),
    )(weights, own, behind1, behind2, ahead1, ahead2)


def exchange(current):
    return (shift(current[1:], 1), shift(current[2:], 2), shift(current[:2], -1), shift(current[:1], -2))


def total_over(pay, axis):
    return jnp.sum(lax.all_to_all(pay, axis, 0, 0, tiled=True), axis=0, keepdims=True)


def body(upper_tiles, listed_mask):
    rows_total = lax.axis_size(AXES)
    here = lax.axis_index(AXES)
    slot_count = upper_tiles.shape[1]
    tile_order = upper_tiles.shape[-1]
    slots = jnp.arange(slot_count, dtype=jnp.int32)
    valid = listed_mask[0] * (here + slots < rows_total).astype(jnp.int32)
    weights = valid.astype(jnp.float32)
    current = upper_tiles[0] * weights[:, None, None]
    current, pay = step(True, weights, current, *exchange(current), lax.axis_size("col"))
    part = total_over(pay, "col")
    part = jnp.broadcast_to(part, (lax.axis_size("row"), LANES))
    traces = total_over(part, "row")[0, :STEPS]
    (purified,) = step(False, weights, current, *exchange(current), 0)
    return (purified[None], traces / tile_order)


def solution(mesh):
    return jax.shard_map(
        body,
        mesh=mesh,
        in_specs=(P(("row", "col"), None, None, None), P(("row", "col"), None)),
        out_specs=(P(("row", "col"), None, None, None), P()),
        check_vma=False,
    )
```

```python
import functools

import jax
import jax.numpy as jnp
from jax import lax
from jax.experimental import pallas as pl
from jax.experimental.pallas import tpu as pltpu
from jax.sharding import PartitionSpec as P

STEPS = 2
AXES = ("row", "col")
LANES = 128
SPREAD_COST = 10**11


def shift(value, steps):
    count = lax.axis_size(AXES)
    first, last = (max(0, -steps), min(count, count - steps))
    return lax.ppermute(value, AXES, [(source, source + steps) for source in range(first, last)])


def split(tile):
    high = tile.astype(jnp.bfloat16)
    return (high, (tile - high.astype(jnp.float32)).astype(jnp.bfloat16))


def product(left, right, left_dim, right_dim):
    def one(a, b):
        return lax.dot_general(
            a, b, (((left_dim,), (right_dim,)), ((), ())), preferred_element_type=jnp.float32
        )

    return one(left[0], right[0]) + (one(left[0], right[1]) + one(left[1], right[0]))


def squared_norm(tiles):
    total = tiles[0] * tiles[0] + 2.0 * (tiles[1] * tiles[1] + tiles[2] * tiles[2])
    return jnp.sum(total)


def step_kernel(even, weights, own, behind1, behind2, ahead1, ahead2, out, *norms):
    own_f = [own[slot] for slot in range(3)]
    c0, c1, c2 = (split(tile) for tile in own_f)
    b10, b11 = (split(behind1[0]), split(behind1[1]))
    b22 = split(behind2[0])
    a10, a11 = (split(ahead1[0]), split(ahead1[1]))
    a20 = split(ahead2[0])
    squares = (
        product(c0, c0, 1, 0)
        + product(c1, c1, 1, 1)
        + product(c2, c2, 1, 1)
        + product(b10, b10, 0, 0)
        + product(b22, b22, 0, 0),
        product(c0, c1, 1, 0)
        + product(c1, a10, 1, 0)
        + product(c2, a11, 1, 1)
        + product(b10, b11, 0, 0),
        product(c0, c2, 1, 0) + product(c1, a11, 1, 0) + product(c2, a20, 1, 0),
    )
    fresh = []
    for slot in range(3):
        value = 2.0 * own_f[slot] - squares[slot] if even else squares[slot]
        fresh.append(value * weights[slot])
        out[slot] = fresh[slot]
    if norms:
        (pay,) = norms
        lane = lax.broadcasted_iota(jnp.int32, pay.shape, 1)
        pay[...] = jnp.where(lane == 0, squared_norm(own_f), squared_norm(fresh))


def step(even, weights, own, behind1, behind2, ahead1, ahead2, pay_rows):
    vmem = pl.BlockSpec(memory_space=pltpu.VMEM)
    shapes = [jax.ShapeDtypeStruct(own.shape, jnp.float32)]
    if pay_rows:
        shapes.append(jax.ShapeDtypeStruct((pay_rows, LANES), jnp.float32))
    order = own.shape[-1]
    return pl.pallas_call(
        functools.partial(step_kernel, even),
        out_shape=shapes,
        in_specs=[pl.BlockSpec(memory_space=pltpu.SMEM)] + [vmem] * 5,
        out_specs=[vmem] * len(shapes),
        compiler_params=pltpu.CompilerParams(vmem_limit_bytes=12 * 1024 * 1024),
        cost_estimate=pl.CostEstimate(
            flops=36 * 2 * order**3, bytes_accessed=12 * 4 * order**2, transcendentals=0
        ),
    )(weights, own, behind1, behind2, ahead1, ahead2)


def exchange(current):
    return (shift(current[1:], 1), shift(current[2:], 2), shift(current[:2], -1), shift(current[:1], -2))


def spread_kernel(parts, out):
    out[...] = jnp.broadcast_to(jnp.sum(parts[...], axis=0, keepdims=True), out.shape)


def spread(parts, rows):
    vmem = pl.BlockSpec(memory_space=pltpu.VMEM)
    return pl.pallas_call(
        spread_kernel,
        out_shape=jax.ShapeDtypeStruct((rows, LANES), jnp.float32),
        in_specs=[vmem],
        out_specs=vmem,
        compiler_params=pltpu.CompilerParams(vmem_limit_bytes=1024 * 1024),
        cost_estimate=pl.CostEstimate(flops=SPREAD_COST, bytes_accessed=0, transcendentals=0),
    )(parts)


def body(upper_tiles, listed_mask):
    rows_total = lax.axis_size(AXES)
    here = lax.axis_index(AXES)
    slot_count = upper_tiles.shape[1]
    tile_order = upper_tiles.shape[-1]
    slots = jnp.arange(slot_count, dtype=jnp.int32)
    valid = listed_mask[0] * (here + slots < rows_total).astype(jnp.int32)
    weights = valid.astype(jnp.float32)
    current = upper_tiles[0] * weights[:, None, None]
    current, pay = step(True, weights, current, *exchange(current), lax.axis_size("col"))
    part = spread(lax.all_to_all(pay, "col", 0, 0, tiled=True), lax.axis_size("row"))
    (purified,) = step(False, weights, current, *exchange(current), 0)
    gathered = lax.all_to_all(part, "row", 0, 0, tiled=True)
    gathered, purified = lax.optimization_barrier((gathered, purified))
    traces = jnp.sum(gathered, axis=0)[:STEPS]
    return (purified[None], traces / tile_order)


def solution(mesh):
    return jax.shard_map(
        body,
        mesh=mesh,
        in_specs=(P(("row", "col"), None, None, None), P(("row", "col"), None)),
        out_specs=(P(("row", "col"), None, None, None), P()),
        check_vma=False,
    )
```

```python
import jax
import jax.numpy as jnp
from jax import lax
from jax.experimental import pallas as pl
from jax.experimental.pallas import tpu as pltpu
from jax.sharding import PartitionSpec as P

STEPS = 2
SLOTS = 3
SPAN = SLOTS - 1
AXES = ("row", "col")
LANES = 128
MARKS = 8
MIB = 1024 * 1024
SPREAD_COST = 0

VMEM = pl.BlockSpec(memory_space=pltpu.VMEM)
ANY = pl.BlockSpec(memory_space=pltpu.HBM)


def shift(value, steps):
    count = lax.axis_size(AXES)
    first, last = (max(0, -steps), min(count, count - steps))
    return lax.ppermute(value, AXES, [(source, source + steps) for source in range(first, last)])


def split(tile):
    high = tile.astype(jnp.bfloat16)
    return (high, (tile - high.astype(jnp.float32)).astype(jnp.bfloat16))


def product(left, right, left_dim, right_dim):
    def one(a, b):
        return lax.dot_general(
            a, b, (((left_dim,), (right_dim,)), ((), ())), preferred_element_type=jnp.float32
        )

    return one(left[0], right[0]) + (one(left[0], right[1]) + one(left[1], right[0]))


def square(tiles, row, column):
    total = None
    for middle in range(max(row, column) - SPAN, min(row, column) + SPAN + 1):
        left = tiles[min(row, middle), max(row, middle)]
        right = tiles[min(middle, column), max(middle, column)]
        term = product(left, right, 1 if row <= middle else 0, 0 if middle <= column else 1)
        total = term if total is None else total + term
    return total


def squared_norm(tiles):
    total = tiles[0] * tiles[0] + 2.0 * (tiles[1] * tiles[1] + tiles[2] * tiles[2])
    return jnp.sum(total)


def mask_kernel(rows_total, mask, upper, low, high, first, last):
    order = upper.shape[-1]
    here = lax.axis_index("row") * lax.axis_size("col") + lax.axis_index("col")
    weights = [
        jnp.where(here + slot < rows_total, mask[0, slot], 0).astype(jnp.float32) for slot in range(SLOTS)
    ]
    line = lax.broadcasted_iota(jnp.int32, (MARKS, order), 0)
    marks = jnp.zeros((MARKS, order), jnp.float32)
    for slot in range(SLOTS):
        marks = jnp.where(line == slot, weights[slot], marks)
    first[order:] = marks
    last[order:] = marks
    tiles = [upper[0, slot] * weights[slot] for slot in range(SLOTS)]
    for slot in range(SPAN):
        low[slot] = tiles[slot]
        high[slot] = tiles[slot + 1]
    first[:order] = tiles[0]
    last[:order] = tiles[SPAN]


def masked(mask, upper):
    order = upper.shape[-1]
    pair = jax.ShapeDtypeStruct((SPAN, order, order), jnp.float32)
    marked = jax.ShapeDtypeStruct((order + MARKS, order), jnp.float32)
    rows_total = lax.axis_size(AXES)
    return pl.pallas_call(
        lambda *refs: mask_kernel(rows_total, *refs),
        out_shape=[pair, pair, marked, marked],
        in_specs=[pl.BlockSpec(memory_space=pltpu.SMEM), VMEM],
        out_specs=[VMEM] * 4,
        compiler_params=pltpu.CompilerParams(vmem_limit_bytes=8 * MIB),
        cost_estimate=pl.CostEstimate(flops=0, bytes_accessed=36 * order**2, transcendentals=0),
    )(mask, upper)


def near_tiles(low, high, behind1, behind2, ahead1, ahead2):
    order = low.shape[-1]
    return {
        (0, 0): low[0],
        (0, 1): high[0],
        (0, 2): high[1],
        (-1, 0): behind1[0],
        (-1, 1): behind1[1],
        (-2, 0): behind2[:order],
        (1, 1): ahead1[0],
        (1, 2): ahead1[1],
        (2, 2): ahead2[:order],
    }


def first_kernel(low, high, first, behind1, behind2, ahead1, ahead2, pay):
    order = low.shape[-1]
    given = near_tiles(low, high, behind1, behind2, ahead1, ahead2)
    tiles = {place: split(tile) for place, tile in given.items()}
    marks = first[order:]
    own = [given[0, slot] for slot in range(SLOTS)]
    fresh = [(2.0 * own[slot] - square(tiles, 0, slot)) * marks[slot : slot + 1] for slot in range(SLOTS)]
    lane = lax.broadcasted_iota(jnp.int32, pay.shape, 1)
    pay[...] = jnp.where(lane == 0, squared_norm(own), squared_norm(fresh))


def second_kernel(
    low, high, first, behind1, behind2, ahead1, ahead2, *refs
):
    sources, out, buffers, arrived = (refs[:4], refs[4], refs[5:9], refs[9])
    copies = [
        pltpu.make_async_copy(source, buffer, arrived.at[index])
        for index, (source, buffer) in enumerate(zip(sources, buffers))
    ]
    for copy in copies:
        copy.start()
    order = low.shape[-1]
    given = near_tiles(low, high, behind1, behind2, ahead1, ahead2)
    for copy in copies:
        copy.wait()
    behind1_rest, behind2_rest, ahead1_rest, ahead2_rest = buffers
    given[-1, -1] = behind1_rest[:order]
    given[-2, -2], given[-2, -1] = (behind2_rest[0], behind2_rest[1])
    given[1, 3] = ahead1_rest[:order]
    given[2, 3], given[2, 4] = (ahead2_rest[0], ahead2_rest[1])
    marks = {0: first[order:], -2: behind2[order:], -1: behind1_rest[order:], 1: ahead1_rest[order:]}
    tiles = {place: split(tile) for place, tile in given.items()}
    later = {}
    for row, column in ((-2, 0), (-1, 0), (-1, 1), (0, 0), (0, 1), (0, 2), (1, 1), (1, 2), (2, 2)):
        value = 2.0 * given[row, column] - square(tiles, row, column)
        slot = column - row
        if slot:
            value = value * marks[row][slot : slot + 1]
        later[row, column] = split(value)
    for slot in range(SLOTS):
        out[slot] = square(later, 0, slot) * marks[0][slot : slot + 1]


def cost(products, order):
    return pl.CostEstimate(flops=products * 6 * order**3, bytes_accessed=48 * order**2, transcendentals=0)


def first_step(low, high, first, *near):
    return pl.pallas_call(
        first_kernel,
        out_shape=jax.ShapeDtypeStruct((lax.axis_size("col"), LANES), jnp.float32),
        in_specs=[VMEM] * 7,
        out_specs=VMEM,
        compiler_params=pltpu.CompilerParams(vmem_limit_bytes=16 * MIB),
        cost_estimate=cost(12, low.shape[-1]),
    )(low, high, first, *near)


def second_step(low, high, first, near, rest):
    order = low.shape[-1]
    return pl.pallas_call(
        second_kernel,
        out_shape=jax.ShapeDtypeStruct((SLOTS, order, order), jnp.float32),
        in_specs=[VMEM] * 7 + [ANY] * 4,
        out_specs=VMEM,
        scratch_shapes=[pltpu.VMEM(source.shape, jnp.float32) for source in rest]
        + [pltpu.SemaphoreType.DMA((len(rest),))],
        compiler_params=pltpu.CompilerParams(vmem_limit_bytes=24 * MIB),
        cost_estimate=cost(48, order),
    )(low, high, first, *near, *rest)


def spread_kernel(parts, out):
    out[...] = jnp.broadcast_to(jnp.sum(parts[...], axis=0, keepdims=True), out.shape)


def spread(parts, rows):
    return pl.pallas_call(
        spread_kernel,
        out_shape=jax.ShapeDtypeStruct((rows, LANES), jnp.float32),
        in_specs=[VMEM],
        out_specs=VMEM,
        compiler_params=pltpu.CompilerParams(vmem_limit_bytes=MIB),
        cost_estimate=pl.CostEstimate(flops=SPREAD_COST, bytes_accessed=0, transcendentals=0),
    )(parts)


def body(upper_tiles, listed_mask):
    low, high, first, last = masked(listed_mask, upper_tiles)
    near = (shift(high, 1), shift(last, 2), shift(low, -1), shift(first, -2))
    rest = (shift(first, 1), shift(low, 2), shift(last, -1), shift(high, -2))
    pay = first_step(low, high, first, *near)
    part = spread(lax.all_to_all(pay, "col", 0, 0, tiled=True), lax.axis_size("row"))
    purified = second_step(low, high, first, near, rest)
    gathered = lax.all_to_all(part, "row", 0, 0, tiled=True)
    gathered, purified = lax.optimization_barrier((gathered, purified))
    traces = jnp.sum(gathered, axis=0)[:STEPS]
    return (purified[None], traces / upper_tiles.shape[-1])


def solution(mesh):
    return jax.shard_map(
        body,
        mesh=mesh,
        in_specs=(P(("row", "col"), None, None, None), P(("row", "col"), None)),
        out_specs=(P(("row", "col"), None, None, None), P()),
        check_vma=False,
    )
```

```python
import jax
import jax.numpy as jnp
from jax import lax
from jax.experimental import pallas as pl
from jax.experimental.pallas import tpu as pltpu
from jax.sharding import PartitionSpec as P

STEPS = 2
SLOTS = 3
SPAN = SLOTS - 1
AXES = ("row", "col")
LANES = 128
ROW_LINES = 8
MARKS = 8
MIB = 1024 * 1024
SPREAD_COST = 10**11

VMEM = pl.BlockSpec(memory_space=pltpu.VMEM)
SMEM = pl.BlockSpec(memory_space=pltpu.SMEM)
ANY = pl.BlockSpec(memory_space=pl.ANY)

BACK = ((0, 0), (0, 1), (1, 1))
FRONT = ((0, 2), (1, 2), (1, 3))


def permute(value, first_shift, second_shift):
    count = lax.axis_size(AXES)
    moves = [(source, source + (second_shift if source % 2 else first_shift)) for source in range(count)]
    return lax.ppermute(value, AXES, [move for move in moves if 0 <= move[1] < count])


def split(tile):
    high = tile.astype(jnp.bfloat16)
    return (high, (tile - high.astype(jnp.float32)).astype(jnp.bfloat16))


def product(left, right, left_dim, right_dim):
    def one(a, b):
        return lax.dot_general(
            a, b, (((left_dim,), (right_dim,)), ((), ())), preferred_element_type=jnp.float32
        )

    return one(left[0], right[0]) + (one(left[0], right[1]) + one(left[1], right[0]))


def square(tiles, row, column):
    total = None
    for middle in range(max(row, column) - SPAN, min(row, column) + SPAN + 1):
        left = tiles[min(row, middle), max(row, middle)]
        right = tiles[min(middle, column), max(middle, column)]
        term = product(left, right, 1 if row <= middle else 0, 0 if middle <= column else 1)
        total = term if total is None else total + term
    return total


def squared_norm(tiles):
    total = 0.0
    for (row, column), tile in tiles.items():
        total = total + (1.0 if row == column else 2.0) * jnp.sum(tile * tile)
    return total


def by_place(kernel):
    second = lax.rem(lax.axis_index("col"), 2)
    for place in range(2):

        @pl.when(second == place)
        def _():
            kernel(place == 1)


def mask_kernel(rows_total, mask, upper, own, two, one):
    order = upper.shape[-1]
    here = lax.axis_index("row") * lax.axis_size("col") + lax.axis_index("col")
    weights = [
        jnp.where(here + slot < rows_total, mask[0, slot], 0).astype(jnp.float32) for slot in range(SLOTS)
    ]
    line = lax.broadcasted_iota(jnp.int32, (MARKS, order), 0)
    marks = jnp.zeros((MARKS, order), jnp.float32)
    for slot in range(SLOTS):
        marks = jnp.where(line == slot, weights[slot], marks)
    own[SLOTS * order :] = marks
    tiles = [upper[0, slot] * weights[slot] for slot in range(SLOTS)]
    for slot in range(SLOTS):
        own[slot * order : (slot + 1) * order] = tiles[slot]

    def messages(second):
        two[0], two[1] = (tiles[1], tiles[2]) if second else (tiles[0], tiles[1])
        one[...] = tiles[0] if second else tiles[2]

    by_place(messages)


def masked(mask, upper):
    order = upper.shape[-1]
    rows_total = lax.axis_size(AXES)
    return pl.pallas_call(
        lambda *refs: mask_kernel(rows_total, *refs),
        out_shape=[
            jax.ShapeDtypeStruct((SLOTS * order + MARKS, order), jnp.float32),
            jax.ShapeDtypeStruct((2, order, order), jnp.float32),
            jax.ShapeDtypeStruct((order, order), jnp.float32),
        ],
        in_specs=[SMEM, VMEM],
        out_specs=[VMEM] * 3,
        compiler_params=pltpu.CompilerParams(vmem_limit_bytes=8 * MIB),
        cost_estimate=pl.CostEstimate(flops=0, bytes_accessed=36 * order**2, transcendentals=0),
    )(mask, upper)


def first_kernel(own, partner, two, one, out, marks, pay):
    order = own.shape[-1]

    def compute(second):
        given = {}
        weights = {}
        for row, held in enumerate((partner, own) if second else (own, partner)):
            for slot in range(SLOTS):
                given[row, row + slot] = held[slot * order : (slot + 1) * order]
                weights[row, row + slot] = held[SLOTS * order + slot : SLOTS * order + slot + 1]
        before = {(row, column): tile for (row, column), tile in given.items() if row == int(second)}
        far = ((-1, 0), (-1, 1), (-2, 0)) if second else ((2, 2), (2, 3), (3, 3))
        given.update(zip(far, (two[0], two[1], one[...])))
        tiles = {place: split(tile) for place, tile in given.items()}
        after = {}
        for index, place in enumerate(BACK if second else FRONT):
            after[place] = (2.0 * given[place] - square(tiles, *place)) * weights[place]
            out[index] = after[place]
            marks[index : index + 1] = weights[place]
        lane = lax.broadcasted_iota(jnp.int32, pay.shape, 1)
        pay[...] = jnp.where(lane == 0, squared_norm(before), squared_norm(after)) / order

    by_place(compute)


def second_kernel(own, partner, far, marks, kept, sent):
    def compute(second):
        here, there = (BACK, FRONT) if second else (FRONT, BACK)
        away = [(row - 2, column - 2) if second else (row + 2, column + 2) for row, column in there]
        tiles = {}
        for places, held in ((here, own), (there, partner), (away, far)):
            for index, place in enumerate(places):
                tiles[place] = split(held[index])
        targets = [sent.at[0], sent.at[1], kept] if second else [kept, sent.at[0], sent.at[1]]
        for index, place in enumerate(here):
            targets[index][...] = square(tiles, *place) * marks[index : index + 1]

    by_place(compute)


def cost(products, order):
    return pl.CostEstimate(flops=products * 6 * order**3, bytes_accessed=48 * order**2, transcendentals=0)


def first_step(own, partner, two, one):
    order = own.shape[-1]
    return pl.pallas_call(
        first_kernel,
        out_shape=[
            jax.ShapeDtypeStruct((SLOTS, order, order), jnp.float32),
            jax.ShapeDtypeStruct((MARKS, order), jnp.float32),
            jax.ShapeDtypeStruct((lax.axis_size("col"), LANES), jnp.float32),
        ],
        in_specs=[VMEM] * 4,
        out_specs=[VMEM] * 3,
        compiler_params=pltpu.CompilerParams(vmem_limit_bytes=16 * MIB),
        cost_estimate=cost(12, order),
    )(own, partner, two, one)


def second_step(own, partner, far, marks):
    order = own.shape[-1]
    return pl.pallas_call(
        second_kernel,
        out_shape=[
            jax.ShapeDtypeStruct((order, order), jnp.float32),
            jax.ShapeDtypeStruct((2, order, order), jnp.float32),
        ],
        in_specs=[VMEM] * 4,
        out_specs=[VMEM] * 2,
        compiler_params=pltpu.CompilerParams(vmem_limit_bytes=16 * MIB),
        cost_estimate=cost(12, order),
    )(own, partner, far, marks)


def join_kernel(kept, received, out):
    second = lax.rem(lax.axis_index("col"), 2)
    out[pl.ds(second, 2)] = received[...]
    out[SPAN - SPAN * second] = kept[...]


def join(kept, received):
    order = kept.shape[-1]
    return pl.pallas_call(
        join_kernel,
        out_shape=jax.ShapeDtypeStruct((SLOTS, order, order), jnp.float32),
        in_specs=[VMEM] * 2,
        out_specs=VMEM,
        compiler_params=pltpu.CompilerParams(vmem_limit_bytes=8 * MIB),
        cost_estimate=pl.CostEstimate(flops=0, bytes_accessed=24 * order**2, transcendentals=0),
    )(kept, received)


def spread_kernel(parts, out):
    total = jnp.sum(parts[...], axis=0, keepdims=True)
    line = lax.broadcasted_iota(jnp.int32, out.shape, 0)
    out[...] = jnp.where(line % ROW_LINES == 0, total, 0.0)


def spread(parts, rows):
    return pl.pallas_call(
        spread_kernel,
        out_shape=jax.ShapeDtypeStruct((rows, LANES), jnp.float32),
        in_specs=[VMEM],
        out_specs=VMEM,
        compiler_params=pltpu.CompilerParams(vmem_limit_bytes=MIB),
        cost_estimate=pl.CostEstimate(flops=SPREAD_COST, bytes_accessed=0, transcendentals=0),
    )(parts)


def body(upper_tiles, listed_mask):
    own, two, one = masked(listed_mask, upper_tiles)
    two, one, partner = (permute(two, -2, 2), permute(one, 3, -3), permute(own, 1, -1))
    fresh, marks, pay = first_step(own, partner, two, one)
    part = spread(lax.all_to_all(pay, "col", 0, 0, tiled=True), ROW_LINES * lax.axis_size("row"))
    part, marks = lax.optimization_barrier((part, marks))
    kept, sent = second_step(fresh, permute(fresh, 1, -1), permute(fresh, 3, -3), marks)
    purified = join(kept, permute(sent, 1, -1))
    gathered = lax.all_to_all(part, "row", 0, 0, tiled=True)
    gathered, purified = lax.optimization_barrier((gathered, purified))
    traces = jnp.sum(gathered[:, :STEPS], axis=0)
    return (purified[None], traces)


def solution(mesh):
    return jax.shard_map(
        body,
        mesh=mesh,
        in_specs=(P(("row", "col"), None, None, None), P(("row", "col"), None)),
        out_specs=(P(("row", "col"), None, None, None), P()),
        check_vma=False,
    )
```

```python
import jax
import jax.numpy as jnp
from jax import lax
from jax.experimental import pallas as pl
from jax.experimental.pallas import tpu as pltpu
from jax.sharding import PartitionSpec as P

STEPS = 2
SLOTS = 3
SPAN = SLOTS - 1
AXES = ("row", "col")
LANES = 128
MARKS = 8
MIB = 1024 * 1024
SPREAD_COST = 10**11

VMEM = pl.BlockSpec(memory_space=pltpu.VMEM)

BACK = ((0, 0), (0, 1), (1, 1))
FRONT = ((0, 2), (1, 2), (1, 3))
NEAR = ((0, 1), (0, 1, 2, 3))
FAR = ((2, 3), (-2, -1))


def permute(value, first_shift, second_shift):
    count = lax.axis_size(AXES)
    moves = [(source, source + (second_shift if source % 2 else first_shift)) for source in range(count)]
    return lax.ppermute(value, AXES, [move for move in moves if 0 <= move[1] < count])


def split(tile):
    high = tile.astype(jnp.bfloat16)
    return (high, (tile - high.astype(jnp.float32)).astype(jnp.bfloat16))


def product(left, right, left_dim, right_dim):
    def one(a, b):
        return lax.dot_general(
            a, b, (((left_dim,), (right_dim,)), ((), ())), preferred_element_type=jnp.float32
        )

    return one(left[0], right[0]) + (one(left[0], right[1]) + one(left[1], right[0]))


def square(tiles, row, column, chosen=None):
    total = None
    for middle in range(max(row, column) - SPAN, min(row, column) + SPAN + 1):
        if chosen is not None and middle not in chosen:
            continue
        left = tiles[min(row, middle), max(row, middle)]
        right = tiles[min(middle, column), max(middle, column)]
        term = product(left, right, 1 if row <= middle else 0, 0 if middle <= column else 1)
        total = term if total is None else total + term
    return total


def squared_norm(tiles):
    total = 0.0
    for (row, column), tile in tiles.items():
        total = total + (1.0 if row == column else 2.0) * jnp.sum(tile * tile)
    return total


def by_place(kernel):
    second = lax.rem(lax.axis_index("col"), 2)
    for place in range(2):

        @pl.when(second == place)
        def _():
            kernel(place == 1)


def mask_kernel(weights, upper, own, two, one):
    order = upper.shape[-1]
    line = lax.broadcasted_iota(jnp.int32, (MARKS, order), 0)
    marks = jnp.zeros((MARKS, order), jnp.float32)
    for slot in range(SLOTS):
        marks = jnp.where(line == slot, weights[:, slot : slot + 1], marks)
    own[SLOTS * order :] = marks
    tiles = [upper[0, slot] * weights[:, slot : slot + 1] for slot in range(SLOTS)]
    for slot in range(SLOTS):
        own[slot * order : (slot + 1) * order] = tiles[slot]

    def messages(second):
        two[0], two[1] = (tiles[1], tiles[2]) if second else (tiles[0], tiles[1])
        one[...] = tiles[0] if second else tiles[2]

    by_place(messages)


def masked(weights, upper):
    order = upper.shape[-1]
    return pl.pallas_call(
        mask_kernel,
        out_shape=[
            jax.ShapeDtypeStruct((SLOTS * order + MARKS, order), jnp.float32),
            jax.ShapeDtypeStruct((2, order, order), jnp.float32),
            jax.ShapeDtypeStruct((order, order), jnp.float32),
        ],
        in_specs=[VMEM] * 2,
        out_specs=[VMEM] * 3,
        compiler_params=pltpu.CompilerParams(vmem_limit_bytes=8 * MIB),
        cost_estimate=pl.CostEstimate(flops=0, bytes_accessed=36 * order**2, transcendentals=0),
    )(weights, upper)


def pair_tiles(own, partner, second):
    order = own.shape[-1]
    return {
        (row, row + slot): held[slot * order : (slot + 1) * order]
        for row, held in enumerate((partner, own) if second else (own, partner))
        for slot in range(SLOTS)
    }


def near_kernel(own, partner, base, marks, norm):
    order = own.shape[-1]

    def compute(second):
        given = pair_tiles(own, partner, second)
        before = {place: tile for place, tile in given.items() if place[0] == int(second)}
        tiles = {place: split(tile) for place, tile in given.items()}
        for index, place in enumerate(BACK if second else FRONT):
            base[index] = 2.0 * given[place] - square(tiles, *place, chosen=NEAR[second])
            held = partner if (place[0] == 0) == second else own
            line = SLOTS * order + place[1] - place[0]
            marks[index : index + 1] = held[line : line + 1]
        norm[...] = jnp.full(norm.shape, squared_norm(before), jnp.float32)

    by_place(compute)


def first_kernel(own, partner, base, marks, norm, two, one, out, pay):
    order = own.shape[-1]

    def compute(second):
        given = {} if second else pair_tiles(own, partner, second)
        far = ((-1, 0), (-1, 1), (-2, 0)) if second else ((2, 2), (2, 3), (3, 3))
        given.update(zip(far, (two[0], two[1], one[...])))
        used = far if second else (*far, (0, 2), (1, 2), (1, 3))
        tiles = {place: split(given[place]) for place in used}
        after = {}
        for index, place in enumerate(BACK if second else FRONT):
            rest = square(tiles, *place, chosen=FAR[second])
            after[place] = (base[index] - rest) * marks[index : index + 1]
            out[index] = after[place]
        lane = lax.broadcasted_iota(jnp.int32, pay.shape, 1)
        pay[...] = jnp.where(lane == 0, norm[:1], squared_norm(after)) / order

    by_place(compute)


def second_kernel(own, partner, far, marks, kept, sent):
    def compute(second):
        here, there = (BACK, FRONT) if second else (FRONT, BACK)
        away = [(row - 2, column - 2) if second else (row + 2, column + 2) for row, column in there]
        tiles = {}
        for places, held in ((here, own), (there, partner), (away, far)):
            for index, place in enumerate(places):
                tiles[place] = split(held[index])
        targets = [sent.at[0], sent.at[1], kept] if second else [kept, sent.at[0], sent.at[1]]
        for index, place in enumerate(here):
            targets[index][...] = square(tiles, *place) * marks[index : index + 1]

    by_place(compute)


def cost(products, order):
    return pl.CostEstimate(flops=products * 6 * order**3, bytes_accessed=48 * order**2, transcendentals=0)


def first_step(own, partner, two, one):
    order = own.shape[-1]
    tiles = jax.ShapeDtypeStruct((SLOTS, order, order), jnp.float32)
    near = pl.pallas_call(
        near_kernel,
        out_shape=[
            tiles,
            jax.ShapeDtypeStruct((MARKS, order), jnp.float32),
            jax.ShapeDtypeStruct((MARKS, LANES), jnp.float32),
        ],
        in_specs=[VMEM] * 2,
        out_specs=[VMEM] * 3,
        compiler_params=pltpu.CompilerParams(vmem_limit_bytes=12 * MIB),
        cost_estimate=cost(9, order),
    )(own, partner)
    fresh, pay = pl.pallas_call(
        first_kernel,
        out_shape=[tiles, jax.ShapeDtypeStruct((lax.axis_size("col"), LANES), jnp.float32)],
        in_specs=[VMEM] * 7,
        out_specs=[VMEM] * 2,
        compiler_params=pltpu.CompilerParams(vmem_limit_bytes=12 * MIB),
        cost_estimate=cost(5, order),
    )(own, partner, *near, two, one)
    return fresh, near[1], pay


def second_step(own, partner, far, marks):
    order = own.shape[-1]
    return pl.pallas_call(
        second_kernel,
        out_shape=[
            jax.ShapeDtypeStruct((order, order), jnp.float32),
            jax.ShapeDtypeStruct((2, order, order), jnp.float32),
        ],
        in_specs=[VMEM] * 4,
        out_specs=[VMEM] * 2,
        compiler_params=pltpu.CompilerParams(vmem_limit_bytes=16 * MIB),
        cost_estimate=cost(12, order),
    )(own, partner, far, marks)


def join_kernel(kept, received, out):
    second = lax.rem(lax.axis_index("col"), 2)
    out[pl.ds(second, 2)] = received[...]
    out[SPAN - SPAN * second] = kept[...]


def join(kept, received):
    order = kept.shape[-1]
    return pl.pallas_call(
        join_kernel,
        out_shape=jax.ShapeDtypeStruct((SLOTS, order, order), jnp.float32),
        in_specs=[VMEM] * 2,
        out_specs=VMEM,
        compiler_params=pltpu.CompilerParams(vmem_limit_bytes=8 * MIB),
        cost_estimate=pl.CostEstimate(flops=0, bytes_accessed=24 * order**2, transcendentals=0),
    )(kept, received)


def spread_kernel(parts, out):
    total = jnp.sum(parts[...], axis=0, keepdims=True)
    out[...] = jnp.broadcast_to(total, out.shape)


def total_kernel(parts, out):
    out[...] = jnp.sum(parts[...], axis=0, keepdims=True)[:, :STEPS]


def total_of(parts):
    return pl.pallas_call(
        total_kernel,
        out_shape=jax.ShapeDtypeStruct((1, STEPS), jnp.float32),
        in_specs=[VMEM],
        out_specs=VMEM,
        compiler_params=pltpu.CompilerParams(vmem_limit_bytes=MIB),
        cost_estimate=pl.CostEstimate(flops=SPREAD_COST, bytes_accessed=0, transcendentals=0),
    )(parts)


def spread(parts, rows):
    return pl.pallas_call(
        spread_kernel,
        out_shape=jax.ShapeDtypeStruct((rows, LANES), jnp.float32),
        in_specs=[VMEM],
        out_specs=VMEM,
        compiler_params=pltpu.CompilerParams(vmem_limit_bytes=MIB),
        cost_estimate=pl.CostEstimate(flops=SPREAD_COST, bytes_accessed=0, transcendentals=0),
    )(parts)


def body(upper_tiles, listed_mask):
    rows_total = lax.axis_size(AXES)
    slots = jnp.arange(SLOTS, dtype=jnp.int32)
    valid = listed_mask * (lax.axis_index(AXES) + slots < rows_total).astype(jnp.int32)
    own, two, one = masked(valid.astype(jnp.float32), upper_tiles)
    two, one, partner = (permute(two, -2, 2), permute(one, 3, -3), permute(own, 1, -1))
    fresh, marks, pay = first_step(own, partner, two, one)
    part = spread(lax.all_to_all(pay, "col", 0, 0, tiled=True), lax.axis_size("row"))
    part, marks = lax.optimization_barrier((part, marks))
    kept, sent = second_step(fresh, permute(fresh, 1, -1), permute(fresh, 3, -3), marks)
    gathered = lax.all_to_all(part, "row", 0, 0, tiled=True)
    total = total_of(gathered)
    kept, total = lax.optimization_barrier((kept, total))
    purified = join(kept, permute(sent, 1, -1))
    traces = total[0]
    return (purified[None], traces)


def solution(mesh):
    return jax.shard_map(
        body,
        mesh=mesh,
        in_specs=(P(("row", "col"), None, None, None), P(("row", "col"), None)),
        out_specs=(P(("row", "col"), None, None, None), P()),
        check_vma=False,
    )
```

```python
import jax
import jax.numpy as jnp
from jax import lax
from jax.experimental import pallas as pl
from jax.experimental.pallas import tpu as pltpu
from jax.sharding import Mesh
from jax.sharding import PartitionSpec as P

STEPS = 2
SLOTS = 3
SPAN = SLOTS - 1
AXES = ("z", "x", "y", "core")
INNER = ("x", "y", "core")
OUTER = "z"
LANES = 128
MARKS = 8
MIB = 1024 * 1024
SPREAD_COST = 10**11

VMEM = pl.BlockSpec(memory_space=pltpu.VMEM)

BACK = ((0, 0), (0, 1), (1, 1))
FRONT = ((0, 2), (1, 2), (1, 3))
NEAR = ((0, 1), (0, 1, 2, 3))
FAR = ((2, 3), (-2, -1))


def permute(value, first_shift, second_shift):
    count = lax.axis_size(AXES)
    moves = [(source, source + (second_shift if source % 2 else first_shift)) for source in range(count)]
    return lax.ppermute(value, AXES, [move for move in moves if 0 <= move[1] < count])


def split(tile):
    high = tile.astype(jnp.bfloat16)
    return (high, (tile - high.astype(jnp.float32)).astype(jnp.bfloat16))


def product(left, right, left_dim, right_dim):
    def one(a, b):
        return lax.dot_general(
            a, b, (((left_dim,), (right_dim,)), ((), ())), preferred_element_type=jnp.float32
        )

    return one(left[0], right[0]) + (one(left[0], right[1]) + one(left[1], right[0]))


def square(tiles, row, column, chosen=None):
    total = None
    for middle in range(max(row, column) - SPAN, min(row, column) + SPAN + 1):
        if chosen is not None and middle not in chosen:
            continue
        left = tiles[min(row, middle), max(row, middle)]
        right = tiles[min(middle, column), max(middle, column)]
        term = product(left, right, 1 if row <= middle else 0, 0 if middle <= column else 1)
        total = term if total is None else total + term
    return total


def squared_norm(tiles):
    total = 0.0
    for (row, column), tile in tiles.items():
        total = total + (1.0 if row == column else 2.0) * jnp.sum(tile * tile)
    return total


def by_place(kernel):
    second = lax.axis_index("core")
    for place in range(2):

        @pl.when(second == place)
        def _():
            kernel(place == 1)


def mask_kernel(weights, upper, own, two, one):
    order = upper.shape[-1]
    line = lax.broadcasted_iota(jnp.int32, (MARKS, order), 0)
    marks = jnp.zeros((MARKS, order), jnp.float32)
    for slot in range(SLOTS):
        marks = jnp.where(line == slot, weights[:, slot : slot + 1], marks)
    own[SLOTS * order :] = marks
    tiles = [upper[0, slot] * weights[:, slot : slot + 1] for slot in range(SLOTS)]
    for slot in range(SLOTS):
        own[slot * order : (slot + 1) * order] = tiles[slot]

    def messages(second):
        two[0], two[1] = (tiles[1], tiles[2]) if second else (tiles[0], tiles[1])
        one[...] = tiles[0] if second else tiles[2]

    by_place(messages)


def masked(weights, upper):
    order = upper.shape[-1]
    return pl.pallas_call(
        mask_kernel,
        out_shape=[
            jax.ShapeDtypeStruct((SLOTS * order + MARKS, order), jnp.float32),
            jax.ShapeDtypeStruct((2, order, order), jnp.float32),
            jax.ShapeDtypeStruct((order, order), jnp.float32),
        ],
        in_specs=[VMEM] * 2,
        out_specs=[VMEM] * 3,
        compiler_params=pltpu.CompilerParams(vmem_limit_bytes=8 * MIB),
        cost_estimate=pl.CostEstimate(flops=0, bytes_accessed=36 * order**2, transcendentals=0),
    )(weights, upper)


def pair_tiles(own, partner, second):
    order = own.shape[-1]
    return {
        (row, row + slot): held[slot * order : (slot + 1) * order]
        for row, held in enumerate((partner, own) if second else (own, partner))
        for slot in range(SLOTS)
    }


def near_kernel(own, partner, base, marks, norm):
    order = own.shape[-1]

    def compute(second):
        given = pair_tiles(own, partner, second)
        before = {place: tile for place, tile in given.items() if place[0] == int(second)}
        tiles = {place: split(tile) for place, tile in given.items()}
        for index, place in enumerate(BACK if second else FRONT):
            base[index] = 2.0 * given[place] - square(tiles, *place, chosen=NEAR[second])
            held = partner if (place[0] == 0) == second else own
            line = SLOTS * order + place[1] - place[0]
            marks[index : index + 1] = held[line : line + 1]
        norm[...] = jnp.full(norm.shape, squared_norm(before), jnp.float32)

    by_place(compute)


def first_kernel(own, partner, base, marks, norm, two, one, out, pay):
    order = own.shape[-1]

    def compute(second):
        given = {} if second else pair_tiles(own, partner, second)
        far = ((-1, 0), (-1, 1), (-2, 0)) if second else ((2, 2), (2, 3), (3, 3))
        given.update(zip(far, (two[0], two[1], one[...])))
        used = far if second else (*far, (0, 2), (1, 2), (1, 3))
        tiles = {place: split(given[place]) for place in used}
        after = {}
        for index, place in enumerate(BACK if second else FRONT):
            rest = square(tiles, *place, chosen=FAR[second])
            after[place] = (base[index] - rest) * marks[index : index + 1]
            out[index] = after[place]
        lane = lax.broadcasted_iota(jnp.int32, pay.shape, 1)
        pay[...] = jnp.where(lane == 0, norm[:1], squared_norm(after)) / order

    by_place(compute)


def second_kernel(own, partner, far, marks, kept, sent):
    def compute(second):
        here, there = (BACK, FRONT) if second else (FRONT, BACK)
        away = [(row - 2, column - 2) if second else (row + 2, column + 2) for row, column in there]
        tiles = {}
        for places, held in ((here, own), (there, partner), (away, far)):
            for index, place in enumerate(places):
                tiles[place] = split(held[index])
        targets = [sent.at[0], sent.at[1], kept] if second else [kept, sent.at[0], sent.at[1]]
        for index, place in enumerate(here):
            targets[index][...] = square(tiles, *place) * marks[index : index + 1]

    by_place(compute)


def cost(products, order):
    return pl.CostEstimate(flops=products * 6 * order**3, bytes_accessed=48 * order**2, transcendentals=0)


def first_step(own, partner, two, one):
    order = own.shape[-1]
    tiles = jax.ShapeDtypeStruct((SLOTS, order, order), jnp.float32)
    near = pl.pallas_call(
        near_kernel,
        out_shape=[
            tiles,
            jax.ShapeDtypeStruct((MARKS, order), jnp.float32),
            jax.ShapeDtypeStruct((MARKS, LANES), jnp.float32),
        ],
        in_specs=[VMEM] * 2,
        out_specs=[VMEM] * 3,
        compiler_params=pltpu.CompilerParams(vmem_limit_bytes=12 * MIB),
        cost_estimate=cost(9, order),
    )(own, partner)
    fresh, pay = pl.pallas_call(
        first_kernel,
        out_shape=[tiles, jax.ShapeDtypeStruct((lax.axis_size(INNER), LANES), jnp.float32)],
        in_specs=[VMEM] * 7,
        out_specs=[VMEM] * 2,
        compiler_params=pltpu.CompilerParams(vmem_limit_bytes=12 * MIB),
        cost_estimate=cost(5, order),
    )(own, partner, *near, two, one)
    return fresh, near[1], pay


def second_step(own, partner, far, marks):
    order = own.shape[-1]
    return pl.pallas_call(
        second_kernel,
        out_shape=[
            jax.ShapeDtypeStruct((order, order), jnp.float32),
            jax.ShapeDtypeStruct((2, order, order), jnp.float32),
        ],
        in_specs=[VMEM] * 4,
        out_specs=[VMEM] * 2,
        compiler_params=pltpu.CompilerParams(vmem_limit_bytes=16 * MIB),
        cost_estimate=cost(12, order),
    )(own, partner, far, marks)


def join_kernel(kept, received, out):
    second = lax.axis_index("core")
    out[pl.ds(second, 2)] = received[...]
    out[SPAN - SPAN * second] = kept[...]


def join(kept, received):
    order = kept.shape[-1]
    return pl.pallas_call(
        join_kernel,
        out_shape=jax.ShapeDtypeStruct((SLOTS, order, order), jnp.float32),
        in_specs=[VMEM] * 2,
        out_specs=VMEM,
        compiler_params=pltpu.CompilerParams(vmem_limit_bytes=8 * MIB),
        cost_estimate=pl.CostEstimate(flops=0, bytes_accessed=24 * order**2, transcendentals=0),
    )(kept, received)


def spread_kernel(parts, out):
    total = jnp.sum(parts[...], axis=0, keepdims=True)
    out[...] = jnp.broadcast_to(total, out.shape)


def total_kernel(parts, out):
    out[...] = jnp.sum(parts[...], axis=0, keepdims=True)[:, :STEPS]


def total_of(parts):
    return pl.pallas_call(
        total_kernel,
        out_shape=jax.ShapeDtypeStruct((1, STEPS), jnp.float32),
        in_specs=[VMEM],
        out_specs=VMEM,
        compiler_params=pltpu.CompilerParams(vmem_limit_bytes=MIB),
        cost_estimate=pl.CostEstimate(flops=SPREAD_COST, bytes_accessed=0, transcendentals=0),
    )(parts)


def spread(parts, rows):
    return pl.pallas_call(
        spread_kernel,
        out_shape=jax.ShapeDtypeStruct((rows, LANES), jnp.float32),
        in_specs=[VMEM],
        out_specs=VMEM,
        compiler_params=pltpu.CompilerParams(vmem_limit_bytes=MIB),
        cost_estimate=pl.CostEstimate(flops=SPREAD_COST, bytes_accessed=0, transcendentals=0),
    )(parts)


def body(upper_tiles, listed_mask):
    rows_total = lax.axis_size(AXES)
    slots = jnp.arange(SLOTS, dtype=jnp.int32)
    valid = listed_mask * (lax.axis_index(AXES) + slots < rows_total).astype(jnp.int32)
    own, two, one = masked(valid.astype(jnp.float32), upper_tiles)
    two, one, partner = (permute(two, -2, 2), permute(one, 3, -3), permute(own, 1, -1))
    fresh, marks, pay = first_step(own, partner, two, one)
    part = spread(lax.all_to_all(pay, INNER, 0, 0, tiled=True), lax.axis_size(OUTER))
    part, marks = lax.optimization_barrier((part, marks))
    kept, sent = second_step(fresh, permute(fresh, 1, -1), permute(fresh, 3, -3), marks)
    gathered = lax.all_to_all(part, OUTER, 0, 0, tiled=True)
    total = total_of(gathered)
    kept, total = lax.optimization_barrier((kept, total))
    purified = join(kept, permute(sent, 1, -1))
    traces = total[0]
    return (purified[None], traces)


def solution(mesh):
    rows, columns = mesh.devices.shape
    parted = Mesh(mesh.devices.reshape(rows // 4, 4, columns // 2, 2), AXES)
    return jax.shard_map(
        body,
        mesh=parted,
        in_specs=(P(AXES), P(AXES)),
        out_specs=(P(AXES), P()),
        check_vma=False,
    )
```

```python
import jax
import jax.numpy as jnp
from jax import lax
from jax.experimental import pallas as pl
from jax.experimental.pallas import tpu as pltpu
from jax.sharding import Mesh
from jax.sharding import PartitionSpec as P

STEPS = 2
SLOTS = 3
SPAN = SLOTS - 1
AXES = ("z", "x", "y", "core")
INNER = ("x", "y", "core")
OUTER = "z"
LANES = 128
MARKS = 8
MIB = 1024 * 1024
SPREAD_COST = 10**11

VMEM = pl.BlockSpec(memory_space=pltpu.VMEM)

BACK = ((0, 0), (0, 1), (1, 1))
FRONT = ((0, 2), (1, 2), (1, 3))
NEAR = ((0, 1), (0, 1, 2, 3))
FAR = ((2, 3), (-2, -1))


def permute(value, first_shift, second_shift):
    count = lax.axis_size(AXES)
    moves = [(source, source + (second_shift if source % 2 else first_shift)) for source in range(count)]
    return lax.ppermute(value, AXES, [move for move in moves if 0 <= move[1] < count])


def split(tile):
    high = tile.astype(jnp.bfloat16)
    return (high, (tile - high.astype(jnp.float32)).astype(jnp.bfloat16))


def product(left, right, left_dim, right_dim):
    def one(a, b):
        return lax.dot_general(
            a, b, (((left_dim,), (right_dim,)), ((), ())), preferred_element_type=jnp.float32
        )

    return one(left[0], right[0]) + (one(left[0], right[1]) + one(left[1], right[0]))


def square(tiles, row, column, chosen=None):
    total = None
    for middle in range(max(row, column) - SPAN, min(row, column) + SPAN + 1):
        if chosen is not None and middle not in chosen:
            continue
        left = tiles[min(row, middle), max(row, middle)]
        right = tiles[min(middle, column), max(middle, column)]
        term = product(left, right, 1 if row <= middle else 0, 0 if middle <= column else 1)
        total = term if total is None else total + term
    return total


def squared_norm(tiles):
    total = 0.0
    for (row, column), tile in tiles.items():
        total = total + (1.0 if row == column else 2.0) * jnp.sum(tile * tile)
    return total


def by_place(kernel):
    second = lax.axis_index("core")
    for place in range(2):

        @pl.when(second == place)
        def _():
            kernel(place == 1)


def mask_kernel(rows_total, mask, upper, own, two, one, held, buffer, arrived):
    order = upper.shape[-1]
    flags = pltpu.make_async_copy(mask, held, arrived.at[SLOTS])
    flags.start()
    copies = [
        pltpu.make_async_copy(upper.at[0, slot], buffer.at[slot], arrived.at[slot]) for slot in range(SLOTS)
    ]
    for copy in copies:
        copy.start()
    here = lax.axis_index(AXES)
    second = lax.axis_index("core")
    line = lax.broadcasted_iota(jnp.int32, (MARKS, order), 0)
    marks = jnp.zeros((MARKS, order), jnp.float32)
    flags.wait()
    weights = [
        jnp.where(here + slot < rows_total, held[0, slot], 0).astype(jnp.float32) for slot in range(SLOTS)
    ]
    for slot in range(SLOTS):
        marks = jnp.where(line == slot, weights[slot], marks)
    own[SLOTS * order :] = marks
    for slot in range(SLOTS):
        copies[slot].wait()
        tile = buffer[slot] * weights[slot]
        own[slot * order : (slot + 1) * order] = tile
        for place in range(2):

            @pl.when(second == place)
            def _():
                if 0 <= slot - place < 2:
                    two[slot - place] = tile
                else:
                    one[...] = tile


def masked(mask, upper):
    order = upper.shape[-1]
    rows_total = lax.axis_size(AXES)
    return pl.pallas_call(
        lambda *refs: mask_kernel(rows_total, *refs),
        out_shape=[
            jax.ShapeDtypeStruct((SLOTS * order + MARKS, order), jnp.float32),
            jax.ShapeDtypeStruct((2, order, order), jnp.float32),
            jax.ShapeDtypeStruct((order, order), jnp.float32),
        ],
        in_specs=[pl.BlockSpec(memory_space=pl.ANY)] * 2,
        out_specs=[VMEM] * 3,
        scratch_shapes=[
            pltpu.SMEM(mask.shape, jnp.int32),
            pltpu.VMEM((SLOTS, order, order), jnp.float32),
            pltpu.SemaphoreType.DMA((SLOTS + 1,)),
        ],
        compiler_params=pltpu.CompilerParams(vmem_limit_bytes=8 * MIB),
        cost_estimate=pl.CostEstimate(flops=0, bytes_accessed=36 * order**2, transcendentals=0),
    )(pltpu.with_memory_space_constraint(mask, pltpu.HBM), pltpu.with_memory_space_constraint(upper, pltpu.HBM))


def pair_tiles(own, partner, second):
    order = own.shape[-1]
    return {
        (row, row + slot): held[slot * order : (slot + 1) * order]
        for row, held in enumerate((partner, own) if second else (own, partner))
        for slot in range(SLOTS)
    }


def near_kernel(own, partner, base, marks, norm):
    order = own.shape[-1]

    def compute(second):
        given = pair_tiles(own, partner, second)
        before = {place: tile for place, tile in given.items() if place[0] == int(second)}
        tiles = {place: split(tile) for place, tile in given.items()}
        for index, place in enumerate(BACK if second else FRONT):
            base[index] = 2.0 * given[place] - square(tiles, *place, chosen=NEAR[second])
            held = partner if (place[0] == 0) == second else own
            line = SLOTS * order + place[1] - place[0]
            marks[index : index + 1] = held[line : line + 1]
        norm[...] = jnp.full(norm.shape, squared_norm(before), jnp.float32)

    by_place(compute)


def first_kernel(own, partner, base, marks, norm, two, one, out, pay):
    order = own.shape[-1]

    def compute(second):
        given = {} if second else pair_tiles(own, partner, second)
        far = ((-1, 0), (-1, 1), (-2, 0)) if second else ((2, 2), (2, 3), (3, 3))
        given.update(zip(far, (two[0], two[1], one[...])))
        used = far if second else (*far, (0, 2), (1, 2), (1, 3))
        tiles = {place: split(given[place]) for place in used}
        after = {}
        for index, place in enumerate(BACK if second else FRONT):
            rest = square(tiles, *place, chosen=FAR[second])
            after[place] = (base[index] - rest) * marks[index : index + 1]
            out[index] = after[place]
        lane = lax.broadcasted_iota(jnp.int32, pay.shape, 1)
        pay[...] = jnp.where(lane == 0, norm[:1], squared_norm(after)) / order

    by_place(compute)


def sides(second):
    here, there = (BACK, FRONT) if second else (FRONT, BACK)
    away = [(row - 2, column - 2) if second else (row + 2, column + 2) for row, column in there]
    return here, there, away


def held_tiles(*groups):
    return {place: split(held[index]) for places, held in groups for index, place in enumerate(places)}


def middle_kernel(own, partner, base):
    def compute(second):
        here, there, _ = sides(second)
        tiles = held_tiles((here, own), (there, partner))
        for index, place in enumerate(here):
            base[index] = square(tiles, *place, chosen=NEAR[second])

    by_place(compute)


def second_kernel(own, partner, base, far, marks, kept, sent):
    def compute(second):
        here, there, away = sides(second)
        tiles = held_tiles((away, far)) if second else held_tiles((here, own), (away, far))
        targets = [sent.at[0], sent.at[1], kept] if second else [kept, sent.at[0], sent.at[1]]
        for index, place in enumerate(here):
            total = base[index] + square(tiles, *place, chosen=FAR[second])
            targets[index][...] = total * marks[index : index + 1]

    by_place(compute)


def cost(products, order):
    return pl.CostEstimate(flops=products * 6 * order**3, bytes_accessed=48 * order**2, transcendentals=0)


def first_step(own, partner, two, one):
    order = own.shape[-1]
    tiles = jax.ShapeDtypeStruct((SLOTS, order, order), jnp.float32)
    near = pl.pallas_call(
        near_kernel,
        out_shape=[
            tiles,
            jax.ShapeDtypeStruct((MARKS, order), jnp.float32),
            jax.ShapeDtypeStruct((MARKS, LANES), jnp.float32),
        ],
        in_specs=[VMEM] * 2,
        out_specs=[VMEM] * 3,
        compiler_params=pltpu.CompilerParams(vmem_limit_bytes=12 * MIB),
        cost_estimate=cost(9, order),
    )(own, partner)
    fresh, pay = pl.pallas_call(
        first_kernel,
        out_shape=[tiles, jax.ShapeDtypeStruct((lax.axis_size(OUTER), LANES), jnp.float32)],
        in_specs=[VMEM] * 7,
        out_specs=[VMEM] * 2,
        compiler_params=pltpu.CompilerParams(vmem_limit_bytes=12 * MIB),
        cost_estimate=cost(5, order),
    )(own, partner, *near, two, one)
    return fresh, near[1], pay


def second_step(own, partner, far, marks):
    order = own.shape[-1]
    base = pl.pallas_call(
        middle_kernel,
        out_shape=jax.ShapeDtypeStruct(own.shape, jnp.float32),
        in_specs=[VMEM] * 2,
        out_specs=VMEM,
        compiler_params=pltpu.CompilerParams(vmem_limit_bytes=12 * MIB),
        cost_estimate=cost(9, order),
    )(own, partner)
    return pl.pallas_call(
        second_kernel,
        out_shape=[
            jax.ShapeDtypeStruct((order, order), jnp.float32),
            jax.ShapeDtypeStruct((2, order, order), jnp.float32),
        ],
        in_specs=[VMEM] * 5,
        out_specs=[VMEM] * 2,
        compiler_params=pltpu.CompilerParams(vmem_limit_bytes=12 * MIB),
        cost_estimate=cost(5, order),
    )(own, partner, base, far, marks)


def join_kernel(kept, received, out, sent):
    second = lax.axis_index("core")
    copies = [
        pltpu.make_async_copy(received, out.at[pl.ds(second, 2)], sent.at[0]),
        pltpu.make_async_copy(kept, out.at[SPAN - SPAN * second], sent.at[1]),
    ]
    for copy in copies:
        copy.start()
    for copy in copies:
        copy.wait()


def join(kept, received):
    order = kept.shape[-1]
    return pl.pallas_call(
        join_kernel,
        out_shape=jax.ShapeDtypeStruct((SLOTS, order, order), jnp.float32),
        in_specs=[VMEM] * 2,
        out_specs=pl.BlockSpec(memory_space=pl.ANY),
        scratch_shapes=[pltpu.SemaphoreType.DMA((2,))],
        compiler_params=pltpu.CompilerParams(vmem_limit_bytes=2 * MIB),
        cost_estimate=pl.CostEstimate(flops=0, bytes_accessed=24 * order**2, transcendentals=0),
    )(kept, received)


def spread_kernel(parts, out):
    total = jnp.sum(parts[...], axis=0, keepdims=True)
    out[...] = jnp.broadcast_to(total, out.shape)


def total_kernel(parts, out):
    out[...] = jnp.sum(parts[...], axis=0, keepdims=True)[:, :STEPS]


def total_of(parts):
    return pl.pallas_call(
        total_kernel,
        out_shape=jax.ShapeDtypeStruct((1, STEPS), jnp.float32),
        in_specs=[VMEM],
        out_specs=VMEM,
        compiler_params=pltpu.CompilerParams(vmem_limit_bytes=MIB),
        cost_estimate=pl.CostEstimate(flops=SPREAD_COST, bytes_accessed=0, transcendentals=0),
    )(parts)


def spread(parts, rows):
    return pl.pallas_call(
        spread_kernel,
        out_shape=jax.ShapeDtypeStruct((rows, LANES), jnp.float32),
        in_specs=[VMEM],
        out_specs=VMEM,
        compiler_params=pltpu.CompilerParams(vmem_limit_bytes=MIB),
        cost_estimate=pl.CostEstimate(flops=SPREAD_COST, bytes_accessed=0, transcendentals=0),
    )(parts)


def body(upper_tiles, listed_mask):
    own, two, one = masked(listed_mask, upper_tiles)
    two, one, partner = (permute(two, -2, 2), permute(one, 3, -3), permute(own, 1, -1))
    fresh, marks, pay = first_step(own, partner, two, one)
    part = spread(lax.all_to_all(pay, OUTER, 0, 0, tiled=True), lax.axis_size(INNER))
    part, marks = lax.optimization_barrier((part, marks))
    kept, sent = second_step(fresh, permute(fresh, 1, -1), permute(fresh, 3, -3), marks)
    gathered = lax.all_to_all(part, INNER, 0, 0, tiled=True)
    total = total_of(gathered)
    kept, total = lax.optimization_barrier((kept, total))
    purified = join(kept, permute(sent, 1, -1))
    traces = total[0]
    return (purified[None], traces)


def solution(mesh):
    rows, columns = mesh.devices.shape
    parted = Mesh(mesh.devices.reshape(rows // 4, 4, columns // 2, 2), AXES)
    return jax.shard_map(
        body,
        mesh=parted,
        in_specs=(P(AXES), P(AXES)),
        out_specs=(P(AXES), P()),
        check_vma=False,
    )
```

```python
import jax
import jax.numpy as jnp
from jax import lax
from jax.experimental import pallas as pl
from jax.experimental.pallas import tpu as pltpu
from jax.sharding import Mesh
from jax.sharding import PartitionSpec as P

STEPS = 2
SLOTS = 3
SPAN = SLOTS - 1
AXES = ("z", "x", "y", "core")
INNER = ("x", "y", "core")
OUTER = "z"
LANES = 128
MARKS = 8
MIB = 1024 * 1024
SPREAD_COST = 10**11

VMEM = pl.BlockSpec(memory_space=pltpu.VMEM)

BACK = ((0, 0), (0, 1), (1, 1))
FRONT = ((0, 2), (1, 2), (1, 3))
NEAR = ((0, 1), (0, 1, 2, 3))
FAR = ((2, 3), (-2, -1))


def permute(value, first_shift, second_shift):
    count = lax.axis_size(AXES)
    moves = [(source, source + (second_shift if source % 2 else first_shift)) for source in range(count)]
    return lax.ppermute(value, AXES, [move for move in moves if 0 <= move[1] < count])


def split(tile):
    high = tile.astype(jnp.bfloat16)
    return (high, (tile - high.astype(jnp.float32)).astype(jnp.bfloat16))


def product(left, right, left_dim, right_dim):
    def one(a, b):
        return lax.dot_general(
            a, b, (((left_dim,), (right_dim,)), ((), ())), preferred_element_type=jnp.float32
        )

    return one(left[0], right[0]) + (one(left[0], right[1]) + one(left[1], right[0]))


def square(tiles, row, column, chosen=None):
    total = None
    for middle in range(max(row, column) - SPAN, min(row, column) + SPAN + 1):
        if chosen is not None and middle not in chosen:
            continue
        left = tiles[min(row, middle), max(row, middle)]
        right = tiles[min(middle, column), max(middle, column)]
        term = product(left, right, 1 if row <= middle else 0, 0 if middle <= column else 1)
        total = term if total is None else total + term
    return total


def squared_norm(tiles):
    total = 0.0
    for (row, column), tile in tiles.items():
        total = total + (1.0 if row == column else 2.0) * jnp.sum(tile * tile)
    return total


def by_place(kernel):
    second = lax.axis_index("core")
    for place in range(2):

        @pl.when(second == place)
        def _():
            kernel(place == 1)


def mask_kernel(rows_total, mask, upper, own, two, one, held, buffer, arrived):
    order = upper.shape[-1]
    flags = pltpu.make_async_copy(mask, held, arrived.at[SLOTS])
    flags.start()
    copies = [
        pltpu.make_async_copy(upper.at[0, slot], buffer.at[slot], arrived.at[slot]) for slot in range(SLOTS)
    ]
    for copy in copies:
        copy.start()
    here = lax.axis_index(AXES)
    second = lax.axis_index("core")
    line = lax.broadcasted_iota(jnp.int32, (MARKS, order), 0)
    marks = jnp.zeros((MARKS, order), jnp.float32)
    flags.wait()
    weights = [
        jnp.where(here + slot < rows_total, held[0, slot], 0).astype(jnp.float32) for slot in range(SLOTS)
    ]
    for slot in range(SLOTS):
        marks = jnp.where(line == slot, weights[slot], marks)
    own[SLOTS * order :] = marks
    for slot in range(SLOTS):
        copies[slot].wait()
        tile = buffer[slot] * weights[slot]
        own[slot * order : (slot + 1) * order] = tile
        for place in range(2):

            @pl.when(second == place)
            def _():
                if 0 <= slot - place < 2:
                    two[slot - place] = tile
                else:
                    one[...] = tile


def masked(mask, upper):
    order = upper.shape[-1]
    rows_total = lax.axis_size(AXES)
    return pl.pallas_call(
        lambda *refs: mask_kernel(rows_total, *refs),
        out_shape=[
            jax.ShapeDtypeStruct((SLOTS * order + MARKS, order), jnp.float32),
            jax.ShapeDtypeStruct((2, order, order), jnp.float32),
            jax.ShapeDtypeStruct((order, order), jnp.float32),
        ],
        in_specs=[pl.BlockSpec(memory_space=pl.ANY)] * 2,
        out_specs=[VMEM] * 3,
        scratch_shapes=[
            pltpu.SMEM(mask.shape, jnp.int32),
            pltpu.VMEM((SLOTS, order, order), jnp.float32),
            pltpu.SemaphoreType.DMA((SLOTS + 1,)),
        ],
        compiler_params=pltpu.CompilerParams(vmem_limit_bytes=8 * MIB),
        cost_estimate=pl.CostEstimate(flops=0, bytes_accessed=36 * order**2, transcendentals=0),
    )(pltpu.with_memory_space_constraint(mask, pltpu.HBM), pltpu.with_memory_space_constraint(upper, pltpu.HBM))


def pair_tiles(own, partner, second):
    order = own.shape[-1]
    return {
        (row, row + slot): held[slot * order : (slot + 1) * order]
        for row, held in enumerate((partner, own) if second else (own, partner))
        for slot in range(SLOTS)
    }


def norm_kernel(own, norm):
    order = own.shape[-1]
    tiles = {(0, slot): own[slot * order : (slot + 1) * order] for slot in range(SLOTS)}
    norm[...] = jnp.full(norm.shape, squared_norm(tiles), jnp.float32)


def near_kernel(own, partner, norm, base, marks):
    order = own.shape[-1]

    def compute(second):
        given = pair_tiles(own, partner, second)
        tiles = {place: split(tile) for place, tile in given.items()}
        for index, place in enumerate(BACK if second else FRONT):
            base[index] = 2.0 * given[place] - square(tiles, *place, chosen=NEAR[second])
            held = partner if (place[0] == 0) == second else own
            line = SLOTS * order + place[1] - place[0]
            marks[index : index + 1] = held[line : line + 1]

    by_place(compute)


def first_kernel(own, partner, base, marks, norm, two, one, out, pay):
    order = own.shape[-1]

    def compute(second):
        given = {} if second else pair_tiles(own, partner, second)
        far = ((-1, 0), (-1, 1), (-2, 0)) if second else ((2, 2), (2, 3), (3, 3))
        given.update(zip(far, (two[0], two[1], one[...])))
        used = far if second else (*far, (0, 2), (1, 2), (1, 3))
        tiles = {place: split(given[place]) for place in used}
        after = {}
        for index, place in enumerate(BACK if second else FRONT):
            rest = square(tiles, *place, chosen=FAR[second])
            after[place] = (base[index] - rest) * marks[index : index + 1]
            out[index] = after[place]
        lane = lax.broadcasted_iota(jnp.int32, pay.shape, 1)
        pay[...] = jnp.where(lane == 0, norm[:1], squared_norm(after)) / order

    by_place(compute)


def sides(second):
    here, there = (BACK, FRONT) if second else (FRONT, BACK)
    away = [(row - 2, column - 2) if second else (row + 2, column + 2) for row, column in there]
    return here, there, away


def held_tiles(*groups):
    return {place: split(held[index]) for places, held in groups for index, place in enumerate(places)}


def middle_kernel(own, partner, base):
    def compute(second):
        here, there, _ = sides(second)
        tiles = held_tiles((here, own), (there, partner))
        for index, place in enumerate(here):
            base[index] = square(tiles, *place, chosen=NEAR[second])

    by_place(compute)


def second_kernel(own, partner, base, far, marks, kept, sent):
    def compute(second):
        here, there, away = sides(second)
        tiles = held_tiles((away, far)) if second else held_tiles((here, own), (away, far))
        targets = [sent.at[0], sent.at[1], kept] if second else [kept, sent.at[0], sent.at[1]]
        for index, place in enumerate(here):
            total = base[index] + square(tiles, *place, chosen=FAR[second])
            targets[index][...] = total * marks[index : index + 1]

    by_place(compute)


def cost(products, order):
    return pl.CostEstimate(flops=products * 6 * order**3, bytes_accessed=48 * order**2, transcendentals=0)


def first_step(own, partner, two, one):
    order = own.shape[-1]
    tiles = jax.ShapeDtypeStruct((SLOTS, order, order), jnp.float32)
    lines = jax.ShapeDtypeStruct((MARKS, LANES), jnp.float32)
    norm = pl.pallas_call(
        norm_kernel,
        out_shape=lines,
        in_specs=[VMEM],
        out_specs=VMEM,
        compiler_params=pltpu.CompilerParams(vmem_limit_bytes=2 * MIB),
        cost_estimate=pl.CostEstimate(flops=SPREAD_COST, bytes_accessed=0, transcendentals=0),
    )(own)
    near = pl.pallas_call(
        near_kernel,
        out_shape=[tiles, jax.ShapeDtypeStruct((MARKS, order), jnp.float32)],
        in_specs=[VMEM] * 3,
        out_specs=[VMEM] * 2,
        compiler_params=pltpu.CompilerParams(vmem_limit_bytes=12 * MIB),
        cost_estimate=cost(9, order),
    )(own, partner, norm)
    fresh, pay = pl.pallas_call(
        first_kernel,
        out_shape=[tiles, jax.ShapeDtypeStruct((lax.axis_size(OUTER), LANES), jnp.float32)],
        in_specs=[VMEM] * 7,
        out_specs=[VMEM] * 2,
        compiler_params=pltpu.CompilerParams(vmem_limit_bytes=12 * MIB),
        cost_estimate=cost(5, order),
    )(own, partner, *near, norm, two, one)
    return fresh, near[1], pay


def second_step(own, partner, far, marks):
    order = own.shape[-1]
    base = pl.pallas_call(
        middle_kernel,
        out_shape=jax.ShapeDtypeStruct(own.shape, jnp.float32),
        in_specs=[VMEM] * 2,
        out_specs=VMEM,
        compiler_params=pltpu.CompilerParams(vmem_limit_bytes=12 * MIB),
        cost_estimate=cost(9, order),
    )(own, partner)
    return pl.pallas_call(
        second_kernel,
        out_shape=[
            jax.ShapeDtypeStruct((order, order), jnp.float32),
            jax.ShapeDtypeStruct((2, order, order), jnp.float32),
        ],
        in_specs=[VMEM] * 5,
        out_specs=[VMEM] * 2,
        compiler_params=pltpu.CompilerParams(vmem_limit_bytes=12 * MIB),
        cost_estimate=cost(5, order),
    )(own, partner, base, far, marks)


def join_kernel(kept, received, out, sent):
    second = lax.axis_index("core")
    copies = [
        pltpu.make_async_copy(received, out.at[pl.ds(second, 2)], sent.at[0]),
        pltpu.make_async_copy(kept, out.at[SPAN - SPAN * second], sent.at[1]),
    ]
    for copy in copies:
        copy.start()
    for copy in copies:
        copy.wait()


def join(kept, received):
    order = kept.shape[-1]
    return pl.pallas_call(
        join_kernel,
        out_shape=jax.ShapeDtypeStruct((SLOTS, order, order), jnp.float32),
        in_specs=[VMEM] * 2,
        out_specs=pl.BlockSpec(memory_space=pl.ANY),
        scratch_shapes=[pltpu.SemaphoreType.DMA((2,))],
        compiler_params=pltpu.CompilerParams(vmem_limit_bytes=2 * MIB),
        cost_estimate=pl.CostEstimate(flops=0, bytes_accessed=24 * order**2, transcendentals=0),
    )(kept, received)


def spread_kernel(parts, out):
    total = jnp.sum(parts[...], axis=0, keepdims=True)
    out[...] = jnp.broadcast_to(total, out.shape)


def total_kernel(parts, out):
    out[...] = jnp.sum(parts[...], axis=0, keepdims=True)[:, :STEPS]


def total_of(parts):
    return pl.pallas_call(
        total_kernel,
        out_shape=jax.ShapeDtypeStruct((1, STEPS), jnp.float32),
        in_specs=[VMEM],
        out_specs=VMEM,
        compiler_params=pltpu.CompilerParams(vmem_limit_bytes=MIB),
        cost_estimate=pl.CostEstimate(flops=SPREAD_COST, bytes_accessed=0, transcendentals=0),
    )(parts)


def spread(parts, rows):
    return pl.pallas_call(
        spread_kernel,
        out_shape=jax.ShapeDtypeStruct((rows, LANES), jnp.float32),
        in_specs=[VMEM],
        out_specs=VMEM,
        compiler_params=pltpu.CompilerParams(vmem_limit_bytes=MIB),
        cost_estimate=pl.CostEstimate(flops=SPREAD_COST, bytes_accessed=0, transcendentals=0),
    )(parts)


def body(upper_tiles, listed_mask):
    own, two, one = masked(listed_mask, upper_tiles)
    two, one, partner = (permute(two, -2, 2), permute(one, 3, -3), permute(own, 1, -1))
    fresh, marks, pay = first_step(own, partner, two, one)
    part = spread(lax.all_to_all(pay, OUTER, 0, 0, tiled=True), lax.axis_size(INNER))
    part, marks = lax.optimization_barrier((part, marks))
    kept, sent = second_step(fresh, permute(fresh, 1, -1), permute(fresh, 3, -3), marks)
    gathered = lax.all_to_all(part, INNER, 0, 0, tiled=True)
    total = total_of(gathered)
    kept, total = lax.optimization_barrier((kept, total))
    purified = join(kept, permute(sent, 1, -1))
    traces = total[0]
    return (purified[None], traces)


def solution(mesh):
    rows, columns = mesh.devices.shape
    parted = Mesh(mesh.devices.reshape(rows // 4, 4, columns // 2, 2), AXES)
    return jax.shard_map(
        body,
        mesh=parted,
        in_specs=(P(AXES), P(AXES)),
        out_specs=(P(AXES), P()),
        check_vma=False,
    )
```

```python
import jax
import jax.numpy as jnp
from jax import lax
from jax.experimental import pallas as pl
from jax.experimental.pallas import tpu as pltpu
from jax.sharding import Mesh
from jax.sharding import PartitionSpec as P

STEPS = 2
SLOTS = 3
SPAN = SLOTS - 1
AXES = ("z", "x", "y", "core")
INNER = ("x", "y", "core")
OUTER = "z"
LANES = 128
MARKS = 8
MIB = 1024 * 1024
SPREAD_COST = 10**11

VMEM = pl.BlockSpec(memory_space=pltpu.VMEM)

BACK = ((0, 0), (0, 1), (1, 1))
FRONT = ((0, 2), (1, 2), (1, 3))
NEAR = ((0, 1), (0, 1, 2, 3))
FAR = ((2, 3), (-2, -1))


def permute(value, first_shift, second_shift):
    count = lax.axis_size(AXES)
    moves = [(source, source + (second_shift if source % 2 else first_shift)) for source in range(count)]
    return lax.ppermute(value, AXES, [move for move in moves if 0 <= move[1] < count])


def split(tile):
    high = tile.astype(jnp.bfloat16)
    return (high, (tile - high.astype(jnp.float32)).astype(jnp.bfloat16))


def product(left, right, left_dim, right_dim):
    def one(a, b):
        return lax.dot_general(
            a, b, (((left_dim,), (right_dim,)), ((), ())), preferred_element_type=jnp.float32
        )

    return one(left[0], right[0]) + (one(left[0], right[1]) + one(left[1], right[0]))


def square(tiles, row, column, chosen=None):
    total = None
    for middle in range(max(row, column) - SPAN, min(row, column) + SPAN + 1):
        if chosen is not None and middle not in chosen:
            continue
        left = tiles[min(row, middle), max(row, middle)]
        right = tiles[min(middle, column), max(middle, column)]
        term = product(left, right, 1 if row <= middle else 0, 0 if middle <= column else 1)
        total = term if total is None else total + term
    return total


def squared_norm(tiles):
    total = 0.0
    for (row, column), tile in tiles.items():
        total = total + (1.0 if row == column else 2.0) * jnp.sum(tile * tile)
    return total


def by_place(kernel):
    second = lax.axis_index("core")
    for place in range(2):

        @pl.when(second == place)
        def _():
            kernel(place == 1)


def mask_kernel(rows_total, mask, upper, own, two, one, held, buffer, arrived):
    order = upper.shape[-1]
    flags = pltpu.make_async_copy(mask, held, arrived.at[SLOTS])
    flags.start()
    copies = [
        pltpu.make_async_copy(upper.at[0, slot], buffer.at[slot], arrived.at[slot]) for slot in range(SLOTS)
    ]
    for copy in copies:
        copy.start()
    here = lax.axis_index(AXES)
    second = lax.axis_index("core")
    line = lax.broadcasted_iota(jnp.int32, (MARKS, order), 0)
    marks = jnp.zeros((MARKS, order), jnp.float32)
    flags.wait()
    weights = [
        jnp.where(here + slot < rows_total, held[0, slot], 0).astype(jnp.float32) for slot in range(SLOTS)
    ]
    for slot in range(SLOTS):
        marks = jnp.where(line == slot, weights[slot], marks)
    own[SLOTS * order :] = marks
    for slot in range(SLOTS):
        copies[slot].wait()
        tile = buffer[slot] * weights[slot]
        own[slot * order : (slot + 1) * order] = tile
        for place in range(2):

            @pl.when(second == place)
            def _():
                if 0 <= slot - place < 2:
                    two[slot - place] = tile
                else:
                    one[...] = tile


def masked(mask, upper):
    order = upper.shape[-1]
    rows_total = lax.axis_size(AXES)
    return pl.pallas_call(
        lambda *refs: mask_kernel(rows_total, *refs),
        out_shape=[
            jax.ShapeDtypeStruct((SLOTS * order + MARKS, order), jnp.float32),
            jax.ShapeDtypeStruct((2, order, order), jnp.float32),
            jax.ShapeDtypeStruct((order, order), jnp.float32),
        ],
        in_specs=[pl.BlockSpec(memory_space=pl.ANY)] * 2,
        out_specs=[VMEM] * 3,
        scratch_shapes=[
            pltpu.SMEM(mask.shape, jnp.int32),
            pltpu.VMEM((SLOTS, order, order), jnp.float32),
            pltpu.SemaphoreType.DMA((SLOTS + 1,)),
        ],
        compiler_params=pltpu.CompilerParams(vmem_limit_bytes=8 * MIB),
        cost_estimate=pl.CostEstimate(flops=0, bytes_accessed=36 * order**2, transcendentals=0),
    )(pltpu.with_memory_space_constraint(mask, pltpu.HBM), pltpu.with_memory_space_constraint(upper, pltpu.HBM))


def pair_tiles(own, partner, second):
    order = own.shape[-1]
    return {
        (row, row + slot): held[slot * order : (slot + 1) * order]
        for row, held in enumerate((partner, own) if second else (own, partner))
        for slot in range(SLOTS)
    }


def norm_kernel(own, two, norm):
    order = own.shape[-1]
    tiles = {(0, slot): own[slot * order : (slot + 1) * order] for slot in range(SLOTS)}
    norm[...] = jnp.full(norm.shape, squared_norm(tiles), jnp.float32)


def near_kernel(own, partner, norm, base, marks):
    order = own.shape[-1]

    def compute(second):
        given = pair_tiles(own, partner, second)
        tiles = {place: split(tile) for place, tile in given.items()}
        for index, place in enumerate(BACK if second else FRONT):
            base[index] = 2.0 * given[place] - square(tiles, *place, chosen=NEAR[second])
            held = partner if (place[0] == 0) == second else own
            line = SLOTS * order + place[1] - place[0]
            marks[index : index + 1] = held[line : line + 1]

    by_place(compute)


def first_kernel(own, partner, base, marks, norm, two, one, out, pay):
    order = own.shape[-1]

    def compute(second):
        given = {} if second else pair_tiles(own, partner, second)
        far = ((-1, 0), (-1, 1), (-2, 0)) if second else ((2, 2), (2, 3), (3, 3))
        given.update(zip(far, (two[0], two[1], one[...])))
        used = far if second else (*far, (0, 2), (1, 2), (1, 3))
        tiles = {place: split(given[place]) for place in used}
        after = {}
        for index, place in enumerate(BACK if second else FRONT):
            rest = square(tiles, *place, chosen=FAR[second])
            after[place] = (base[index] - rest) * marks[index : index + 1]
            out[index] = after[place]
        lane = lax.broadcasted_iota(jnp.int32, pay.shape, 1)
        pay[...] = jnp.where(lane == 0, norm[:1], squared_norm(after)) / order

    by_place(compute)


def sides(second):
    here, there = (BACK, FRONT) if second else (FRONT, BACK)
    away = [(row - 2, column - 2) if second else (row + 2, column + 2) for row, column in there]
    return here, there, away


def held_tiles(*groups):
    return {place: split(held[index]) for places, held in groups for index, place in enumerate(places)}


def middle_kernel(own, partner, base):
    def compute(second):
        here, there, _ = sides(second)
        tiles = held_tiles((here, own), (there, partner))
        for index, place in enumerate(here):
            base[index] = square(tiles, *place, chosen=NEAR[second])

    by_place(compute)


def second_kernel(own, partner, base, far, marks, kept, sent):
    def compute(second):
        here, there, away = sides(second)
        tiles = held_tiles((away, far)) if second else held_tiles((here, own), (away, far))
        targets = [sent.at[0], sent.at[1], kept] if second else [kept, sent.at[0], sent.at[1]]
        for index, place in enumerate(here):
            total = base[index] + square(tiles, *place, chosen=FAR[second])
            targets[index][...] = total * marks[index : index + 1]

    by_place(compute)


def cost(products, order):
    return pl.CostEstimate(flops=products * 6 * order**3, bytes_accessed=48 * order**2, transcendentals=0)


def first_step(own, partner, two, one):
    order = own.shape[-1]
    tiles = jax.ShapeDtypeStruct((SLOTS, order, order), jnp.float32)
    lines = jax.ShapeDtypeStruct((MARKS, LANES), jnp.float32)
    norm = pl.pallas_call(
        norm_kernel,
        out_shape=lines,
        in_specs=[VMEM] * 2,
        out_specs=VMEM,
        compiler_params=pltpu.CompilerParams(vmem_limit_bytes=2 * MIB),
        cost_estimate=pl.CostEstimate(flops=SPREAD_COST, bytes_accessed=0, transcendentals=0),
    )(own, two)
    near = pl.pallas_call(
        near_kernel,
        out_shape=[tiles, jax.ShapeDtypeStruct((MARKS, order), jnp.float32)],
        in_specs=[VMEM] * 3,
        out_specs=[VMEM] * 2,
        compiler_params=pltpu.CompilerParams(vmem_limit_bytes=12 * MIB),
        cost_estimate=cost(9, order),
    )(own, partner, norm)
    fresh, pay = pl.pallas_call(
        first_kernel,
        out_shape=[tiles, jax.ShapeDtypeStruct((lax.axis_size(OUTER), LANES), jnp.float32)],
        in_specs=[VMEM] * 7,
        out_specs=[VMEM] * 2,
        compiler_params=pltpu.CompilerParams(vmem_limit_bytes=12 * MIB),
        cost_estimate=cost(5, order),
    )(own, partner, *near, norm, two, one)
    return fresh, near[1], pay


def second_step(own, partner, far, marks):
    order = own.shape[-1]
    base = pl.pallas_call(
        middle_kernel,
        out_shape=jax.ShapeDtypeStruct(own.shape, jnp.float32),
        in_specs=[VMEM] * 2,
        out_specs=VMEM,
        compiler_params=pltpu.CompilerParams(vmem_limit_bytes=12 * MIB),
        cost_estimate=cost(9, order),
    )(own, partner)
    return pl.pallas_call(
        second_kernel,
        out_shape=[
            jax.ShapeDtypeStruct((order, order), jnp.float32),
            jax.ShapeDtypeStruct((2, order, order), jnp.float32),
        ],
        in_specs=[VMEM] * 5,
        out_specs=[VMEM] * 2,
        compiler_params=pltpu.CompilerParams(vmem_limit_bytes=12 * MIB),
        cost_estimate=cost(5, order),
    )(own, partner, base, far, marks)


def join_kernel(kept, received, out, sent):
    second = lax.axis_index("core")
    copies = [
        pltpu.make_async_copy(received, out.at[pl.ds(second, 2)], sent.at[0]),
        pltpu.make_async_copy(kept, out.at[SPAN - SPAN * second], sent.at[1]),
    ]
    for copy in copies:
        copy.start()
    for copy in copies:
        copy.wait()


def join(kept, received):
    order = kept.shape[-1]
    return pl.pallas_call(
        join_kernel,
        out_shape=jax.ShapeDtypeStruct((SLOTS, order, order), jnp.float32),
        in_specs=[VMEM] * 2,
        out_specs=pl.BlockSpec(memory_space=pl.ANY),
        scratch_shapes=[pltpu.SemaphoreType.DMA((2,))],
        compiler_params=pltpu.CompilerParams(vmem_limit_bytes=2 * MIB),
        cost_estimate=pl.CostEstimate(flops=0, bytes_accessed=24 * order**2, transcendentals=0),
    )(kept, received)


def spread_kernel(parts, out):
    total = jnp.sum(parts[...], axis=0, keepdims=True)
    out[...] = jnp.broadcast_to(total, out.shape)


def total_kernel(parts, out):
    out[...] = jnp.sum(parts[...], axis=0, keepdims=True)[:, :STEPS]


def total_of(parts):
    return pl.pallas_call(
        total_kernel,
        out_shape=jax.ShapeDtypeStruct((1, STEPS), jnp.float32),
        in_specs=[VMEM],
        out_specs=VMEM,
        compiler_params=pltpu.CompilerParams(vmem_limit_bytes=MIB),
        cost_estimate=pl.CostEstimate(flops=SPREAD_COST, bytes_accessed=0, transcendentals=0),
    )(parts)


def spread(parts, rows):
    return pl.pallas_call(
        spread_kernel,
        out_shape=jax.ShapeDtypeStruct((rows, LANES), jnp.float32),
        in_specs=[VMEM],
        out_specs=VMEM,
        compiler_params=pltpu.CompilerParams(vmem_limit_bytes=MIB),
        cost_estimate=pl.CostEstimate(flops=SPREAD_COST, bytes_accessed=0, transcendentals=0),
    )(parts)


def body(upper_tiles, listed_mask):
    own, two, one = masked(listed_mask, upper_tiles)
    two, one, partner = (permute(two, -2, 2), permute(one, 3, -3), permute(own, 1, -1))
    fresh, marks, pay = first_step(own, partner, two, one)
    part = spread(lax.all_to_all(pay, OUTER, 0, 0, tiled=True), lax.axis_size(INNER))
    part, marks = lax.optimization_barrier((part, marks))
    kept, sent = second_step(fresh, permute(fresh, 1, -1), permute(fresh, 3, -3), marks)
    gathered = lax.all_to_all(part, INNER, 0, 0, tiled=True)
    total = total_of(gathered)
    kept, total = lax.optimization_barrier((kept, total))
    purified = join(kept, permute(sent, 1, -1))
    traces = total[0]
    return (purified[None], traces)


def solution(mesh):
    rows, columns = mesh.devices.shape
    parted = Mesh(mesh.devices.reshape(rows // 4, 4, columns // 2, 2), AXES)
    return jax.shard_map(
        body,
        mesh=parted,
        in_specs=(P(AXES), P(AXES)),
        out_specs=(P(AXES), P()),
        check_vma=False,
    )
```

```python
import jax
import jax.numpy as jnp
from jax import lax
from jax.experimental import pallas as pl
from jax.experimental.pallas import tpu as pltpu
from jax.sharding import Mesh
from jax.sharding import PartitionSpec as P

STEPS = 2
SLOTS = 3
SPAN = SLOTS - 1
AXES = ("z", "x", "y", "core")
INNER = ("x", "y")
OUTER = ("z", "core")
LANES = 128
MARKS = 8
MIB = 1024 * 1024
SPREAD_COST = 10**11

VMEM = pl.BlockSpec(memory_space=pltpu.VMEM)

BACK = ((0, 0), (0, 1), (1, 1))
FRONT = ((0, 2), (1, 2), (1, 3))
NEAR = ((0, 1, 2, 3), (0, 1))
FAR = ((-2, -1), (2, 3))


def permute(value, first_shift, second_shift):
    count = lax.axis_size(AXES)
    moves = [(source, source + (second_shift if source % 2 else first_shift)) for source in range(count)]
    return lax.ppermute(value, AXES, [move for move in moves if 0 <= move[1] < count])


def split(tile):
    high = tile.astype(jnp.bfloat16)
    return (high, (tile - high.astype(jnp.float32)).astype(jnp.bfloat16))


def product(left, right, left_dim, right_dim):
    def one(a, b):
        return lax.dot_general(
            a, b, (((left_dim,), (right_dim,)), ((), ())), preferred_element_type=jnp.float32
        )

    return one(left[0], right[0]) + (one(left[0], right[1]) + one(left[1], right[0]))


def square(tiles, row, column, chosen=None):
    total = None
    for middle in range(max(row, column) - SPAN, min(row, column) + SPAN + 1):
        if chosen is not None and middle not in chosen:
            continue
        left = tiles[min(row, middle), max(row, middle)]
        right = tiles[min(middle, column), max(middle, column)]
        term = product(left, right, 1 if row <= middle else 0, 0 if middle <= column else 1)
        total = term if total is None else total + term
    return total


def squared_norm(tiles):
    total = 0.0
    for (row, column), tile in tiles.items():
        total = total + (1.0 if row == column else 2.0) * jnp.sum(tile * tile)
    return total


def by_place(kernel):
    second = lax.axis_index("core")
    for place in range(2):

        @pl.when(second == place)
        def _():
            kernel(place == 1)


def mask_kernel(rows_total, mask, upper, own, two, one, held, buffer, arrived):
    order = upper.shape[-1]
    flags = pltpu.make_async_copy(mask, held, arrived.at[SLOTS])
    flags.start()
    copies = [
        pltpu.make_async_copy(upper.at[0, slot], buffer.at[slot], arrived.at[slot]) for slot in range(SLOTS)
    ]
    for copy in copies:
        copy.start()
    here = lax.axis_index(AXES)
    second = lax.axis_index("core")
    line = lax.broadcasted_iota(jnp.int32, (MARKS, order), 0)
    marks = jnp.zeros((MARKS, order), jnp.float32)
    flags.wait()
    weights = [
        jnp.where(here + slot < rows_total, held[0, slot], 0).astype(jnp.float32) for slot in range(SLOTS)
    ]
    for slot in range(SLOTS):
        marks = jnp.where(line == slot, weights[slot], marks)
    own[SLOTS * order :] = marks
    for slot in range(SLOTS):
        copies[slot].wait()
        tile = buffer[slot] * weights[slot]
        own[slot * order : (slot + 1) * order] = tile
        for place in range(2):

            @pl.when(second == place)
            def _():
                if 0 <= slot - place < 2:
                    two[slot - place] = tile
                else:
                    one[...] = tile


def masked(mask, upper):
    order = upper.shape[-1]
    rows_total = lax.axis_size(AXES)
    return pl.pallas_call(
        lambda *refs: mask_kernel(rows_total, *refs),
        out_shape=[
            jax.ShapeDtypeStruct((SLOTS * order + MARKS, order), jnp.float32),
            jax.ShapeDtypeStruct((2, order, order), jnp.float32),
            jax.ShapeDtypeStruct((order, order), jnp.float32),
        ],
        in_specs=[pl.BlockSpec(memory_space=pl.ANY)] * 2,
        out_specs=[VMEM] * 3,
        scratch_shapes=[
            pltpu.SMEM(mask.shape, jnp.int32),
            pltpu.VMEM((SLOTS, order, order), jnp.float32),
            pltpu.SemaphoreType.DMA((SLOTS + 1,)),
        ],
        compiler_params=pltpu.CompilerParams(vmem_limit_bytes=8 * MIB),
        cost_estimate=pl.CostEstimate(flops=0, bytes_accessed=36 * order**2, transcendentals=0),
    )(pltpu.with_memory_space_constraint(mask, pltpu.HBM), pltpu.with_memory_space_constraint(upper, pltpu.HBM))


def pair_tiles(own, partner, second):
    order = own.shape[-1]
    return {
        (row, row + slot): held[slot * order : (slot + 1) * order]
        for row, held in enumerate((partner, own) if second else (own, partner))
        for slot in range(SLOTS)
    }


def norm_kernel(own, two, norm):
    order = own.shape[-1]
    tiles = {(0, slot): own[slot * order : (slot + 1) * order] for slot in range(SLOTS)}
    norm[...] = jnp.full(norm.shape, squared_norm(tiles), jnp.float32)


def near_kernel(own, partner, norm, base, marks):
    order = own.shape[-1]

    def compute(second):
        given = pair_tiles(own, partner, second)
        tiles = {place: split(tile) for place, tile in given.items()}
        for index, place in enumerate(FRONT if second else BACK):
            base[index] = 2.0 * given[place] - square(tiles, *place, chosen=NEAR[second])
            held = partner if (place[0] == 0) == second else own
            line = SLOTS * order + place[1] - place[0]
            marks[index : index + 1] = held[line : line + 1]

    by_place(compute)


def first_kernel(own, partner, base, marks, norm, two, one, out, pay):
    order = own.shape[-1]

    def compute(second):
        given = pair_tiles(own, partner, second) if second else {}
        far = ((2, 2), (2, 3), (3, 3)) if second else ((-1, 0), (-1, 1), (-2, 0))
        given.update(zip(far, (two[0], two[1], one[...])))
        used = (*far, (0, 2), (1, 2), (1, 3)) if second else far
        tiles = {place: split(given[place]) for place in used}
        after = {}
        for index, place in enumerate(FRONT if second else BACK):
            rest = square(tiles, *place, chosen=FAR[second])
            after[place] = (base[index] - rest) * marks[index : index + 1]
            out[index] = after[place]
        lane = lax.broadcasted_iota(jnp.int32, pay.shape, 1)
        pay[...] = jnp.where(lane == 0, norm[:1], squared_norm(after)) / order

    by_place(compute)


def sides(second):
    here, there = (FRONT, BACK) if second else (BACK, FRONT)
    away = [(row + 2, column + 2) if second else (row - 2, column - 2) for row, column in there]
    return here, there, away


def held_tiles(*groups):
    return {place: split(held[index]) for places, held in groups for index, place in enumerate(places)}


def middle_kernel(own, partner, base):
    def compute(second):
        here, there, _ = sides(second)
        tiles = held_tiles((here, own), (there, partner))
        for index, place in enumerate(here):
            base[index] = square(tiles, *place, chosen=NEAR[second])

    by_place(compute)


def second_kernel(own, partner, base, far, marks, kept, sent):
    def compute(second):
        here, there, away = sides(second)
        tiles = held_tiles((here, own), (away, far)) if second else held_tiles((away, far))
        targets = [sent, kept.at[0], kept.at[1]] if second else [kept.at[0], kept.at[1], sent]
        for index, place in enumerate(here):
            total = base[index] + square(tiles, *place, chosen=FAR[second])
            targets[index][...] = total * marks[index : index + 1]

    by_place(compute)


def cost(products, order):
    return pl.CostEstimate(flops=products * 6 * order**3, bytes_accessed=48 * order**2, transcendentals=0)


def first_step(own, partner, two, one):
    order = own.shape[-1]
    tiles = jax.ShapeDtypeStruct((SLOTS, order, order), jnp.float32)
    lines = jax.ShapeDtypeStruct((MARKS, LANES), jnp.float32)
    norm = pl.pallas_call(
        norm_kernel,
        out_shape=lines,
        in_specs=[VMEM] * 2,
        out_specs=VMEM,
        compiler_params=pltpu.CompilerParams(vmem_limit_bytes=2 * MIB),
        cost_estimate=pl.CostEstimate(flops=SPREAD_COST, bytes_accessed=0, transcendentals=0),
    )(own, two)
    near = pl.pallas_call(
        near_kernel,
        out_shape=[tiles, jax.ShapeDtypeStruct((MARKS, order), jnp.float32)],
        in_specs=[VMEM] * 3,
        out_specs=[VMEM] * 2,
        compiler_params=pltpu.CompilerParams(vmem_limit_bytes=12 * MIB),
        cost_estimate=cost(9, order),
    )(own, partner, norm)
    fresh, pay = pl.pallas_call(
        first_kernel,
        out_shape=[tiles, jax.ShapeDtypeStruct((lax.axis_size(OUTER), LANES), jnp.float32)],
        in_specs=[VMEM] * 7,
        out_specs=[VMEM] * 2,
        compiler_params=pltpu.CompilerParams(vmem_limit_bytes=12 * MIB),
        cost_estimate=cost(5, order),
    )(own, partner, *near, norm, two, one)
    return fresh, near[1], pay


def second_step(own, partner, far, marks):
    order = own.shape[-1]
    base = pl.pallas_call(
        middle_kernel,
        out_shape=jax.ShapeDtypeStruct(own.shape, jnp.float32),
        in_specs=[VMEM] * 2,
        out_specs=VMEM,
        compiler_params=pltpu.CompilerParams(vmem_limit_bytes=12 * MIB),
        cost_estimate=cost(9, order),
    )(own, partner)
    return pl.pallas_call(
        second_kernel,
        out_shape=[
            jax.ShapeDtypeStruct((2, order, order), jnp.float32),
            jax.ShapeDtypeStruct((order, order), jnp.float32),
        ],
        in_specs=[VMEM] * 5,
        out_specs=[VMEM] * 2,
        compiler_params=pltpu.CompilerParams(vmem_limit_bytes=12 * MIB),
        cost_estimate=cost(5, order),
    )(own, partner, base, far, marks)


def join_kernel(kept, received, out, sent):
    second = lax.axis_index("core")
    copies = [
        pltpu.make_async_copy(kept, out.at[pl.ds(second, 2)], sent.at[0]),
        pltpu.make_async_copy(received, out.at[SPAN - SPAN * second], sent.at[1]),
    ]
    for copy in copies:
        copy.start()
    for copy in copies:
        copy.wait()


def join(kept, received):
    order = kept.shape[-1]
    return pl.pallas_call(
        join_kernel,
        out_shape=jax.ShapeDtypeStruct((SLOTS, order, order), jnp.float32),
        in_specs=[VMEM] * 2,
        out_specs=pl.BlockSpec(memory_space=pl.ANY),
        scratch_shapes=[pltpu.SemaphoreType.DMA((2,))],
        compiler_params=pltpu.CompilerParams(vmem_limit_bytes=2 * MIB),
        cost_estimate=pl.CostEstimate(flops=0, bytes_accessed=24 * order**2, transcendentals=0),
    )(kept, received)


def spread_kernel(parts, out):
    total = jnp.sum(parts[...], axis=0, keepdims=True)
    out[...] = jnp.broadcast_to(total, out.shape)


def total_kernel(parts, out):
    out[...] = jnp.sum(parts[...], axis=0, keepdims=True)[:, :STEPS]


def total_of(parts):
    return pl.pallas_call(
        total_kernel,
        out_shape=jax.ShapeDtypeStruct((1, STEPS), jnp.float32),
        in_specs=[VMEM],
        out_specs=VMEM,
        compiler_params=pltpu.CompilerParams(vmem_limit_bytes=MIB),
        cost_estimate=pl.CostEstimate(flops=SPREAD_COST, bytes_accessed=0, transcendentals=0),
    )(parts)


def spread(parts, rows):
    return pl.pallas_call(
        spread_kernel,
        out_shape=jax.ShapeDtypeStruct((rows, LANES), jnp.float32),
        in_specs=[VMEM],
        out_specs=VMEM,
        compiler_params=pltpu.CompilerParams(vmem_limit_bytes=MIB),
        cost_estimate=pl.CostEstimate(flops=SPREAD_COST, bytes_accessed=0, transcendentals=0),
    )(parts)


def body(upper_tiles, listed_mask):
    own, two, one = masked(listed_mask, upper_tiles)
    two, one, partner = (permute(two, -1, 1), permute(one, 2, -2), permute(own, 1, -1))
    fresh, marks, pay = first_step(own, partner, two, one)
    part = spread(lax.all_to_all(pay, OUTER, 0, 0, tiled=True), lax.axis_size(INNER))
    part, marks = lax.optimization_barrier((part, marks))
    kept, sent = second_step(fresh, permute(fresh, 1, -1), permute(fresh, -1, 1), marks)
    gathered = lax.all_to_all(part, INNER, 0, 0, tiled=True)
    total = total_of(gathered)
    kept, total = lax.optimization_barrier((kept, total))
    purified = join(kept, permute(sent, 1, -1))
    traces = total[0]
    return (purified[None], traces)


def solution(mesh):
    rows, columns = mesh.devices.shape
    parted = Mesh(mesh.devices.reshape(rows // 4, 4, columns // 2, 2), AXES)
    return jax.shard_map(
        body,
        mesh=parted,
        in_specs=(P(AXES), P(AXES)),
        out_specs=(P(AXES), P()),
        check_vma=False,
    )
```

```python
import jax
import jax.numpy as jnp
from jax import lax
from jax.experimental import pallas as pl
from jax.experimental.pallas import tpu as pltpu
from jax.sharding import Mesh
from jax.sharding import PartitionSpec as P

STEPS = 2
SLOTS = 3
SPAN = SLOTS - 1
AXES = ("z", "x", "y", "core")
INNER = ("x", "y")
OUTER = ("z", "core")
LANES = 128
MARKS = 8
MIB = 1024 * 1024
SPREAD_COST = 10**11

VMEM = pl.BlockSpec(memory_space=pltpu.VMEM)

BACK = ((0, 0), (0, 1), (1, 1))
FRONT = ((0, 2), (1, 2), (1, 3))
NEAR = ((0, 1, 2, 3), (0, 1))
FAR = ((-2, -1), (2, 3))


def permute(value, first_shift, second_shift):
    count = lax.axis_size(AXES)
    moves = [(source, source + (second_shift if source % 2 else first_shift)) for source in range(count)]
    return lax.ppermute(value, AXES, [move for move in moves if 0 <= move[1] < count])


def split(tile):
    high = tile.astype(jnp.bfloat16)
    return (high, (tile - high.astype(jnp.float32)).astype(jnp.bfloat16))


def product(left, right, left_dim, right_dim):
    def one(a, b):
        return lax.dot_general(
            a, b, (((left_dim,), (right_dim,)), ((), ())), preferred_element_type=jnp.float32
        )

    return one(left[0], right[0]) + (one(left[0], right[1]) + one(left[1], right[0]))


def square(tiles, row, column, chosen=None):
    total = None
    for middle in range(max(row, column) - SPAN, min(row, column) + SPAN + 1):
        if chosen is not None and middle not in chosen:
            continue
        left = tiles[min(row, middle), max(row, middle)]
        right = tiles[min(middle, column), max(middle, column)]
        term = product(left, right, 1 if row <= middle else 0, 0 if middle <= column else 1)
        total = term if total is None else total + term
    return total


def squared_norm(tiles):
    total = 0.0
    for (row, column), tile in tiles.items():
        total = total + (1.0 if row == column else 2.0) * jnp.sum(tile * tile)
    return total


def by_place(kernel):
    second = lax.axis_index("core")
    for place in range(2):

        @pl.when(second == place)
        def _():
            kernel(place == 1)


def mask_kernel(rows_total, mask, upper, own, two, one, held, buffer, arrived):
    order = upper.shape[-1]
    flags = pltpu.make_async_copy(mask, held, arrived.at[SLOTS])
    flags.start()
    copies = [
        pltpu.make_async_copy(upper.at[0, slot], buffer.at[slot], arrived.at[slot]) for slot in range(SLOTS)
    ]
    for copy in copies:
        copy.start()
    here = lax.axis_index(AXES)
    second = lax.axis_index("core")
    line = lax.broadcasted_iota(jnp.int32, (MARKS, order), 0)
    marks = jnp.zeros((MARKS, order), jnp.float32)
    flags.wait()
    weights = [
        jnp.where(here + slot < rows_total, held[0, slot], 0).astype(jnp.float32) for slot in range(SLOTS)
    ]
    for slot in range(SLOTS):
        marks = jnp.where(line == slot, weights[slot], marks)
    own[SLOTS * order :] = marks
    for slot in range(SLOTS):
        copies[slot].wait()
        tile = buffer[slot] * weights[slot]
        own[slot * order : (slot + 1) * order] = tile
        for place in range(2):

            @pl.when(second == place)
            def _():
                if 0 <= slot - place < 2:
                    two[slot - place] = tile
                else:
                    one[...] = tile


def masked(mask, upper):
    order = upper.shape[-1]
    rows_total = lax.axis_size(AXES)
    return pl.pallas_call(
        lambda *refs: mask_kernel(rows_total, *refs),
        out_shape=[
            jax.ShapeDtypeStruct((SLOTS * order + MARKS, order), jnp.float32),
            jax.ShapeDtypeStruct((2, order, order), jnp.float32),
            jax.ShapeDtypeStruct((order, order), jnp.float32),
        ],
        in_specs=[pl.BlockSpec(memory_space=pl.ANY)] * 2,
        out_specs=[VMEM] * 3,
        scratch_shapes=[
            pltpu.SMEM(mask.shape, jnp.int32),
            pltpu.VMEM((SLOTS, order, order), jnp.float32),
            pltpu.SemaphoreType.DMA((SLOTS + 1,)),
        ],
        compiler_params=pltpu.CompilerParams(vmem_limit_bytes=8 * MIB),
        cost_estimate=pl.CostEstimate(flops=0, bytes_accessed=36 * order**2, transcendentals=0),
    )(pltpu.with_memory_space_constraint(mask, pltpu.HBM), pltpu.with_memory_space_constraint(upper, pltpu.HBM))


def pair_tiles(own, partner, second):
    order = own.shape[-1]
    return {
        (row, row + slot): held[slot * order : (slot + 1) * order]
        for row, held in enumerate((partner, own) if second else (own, partner))
        for slot in range(SLOTS)
    }


def norm_kernel(own, norm):
    order = own.shape[-1]
    tiles = {(0, slot): own[slot * order : (slot + 1) * order] for slot in range(SLOTS)}
    norm[...] = jnp.full(norm.shape, squared_norm(tiles), jnp.float32)


def near_kernel(own, partner, norm, base, marks):
    order = own.shape[-1]

    def compute(second):
        given = pair_tiles(own, partner, second)
        tiles = {place: split(tile) for place, tile in given.items()}
        for index, place in enumerate(FRONT if second else BACK):
            base[index] = 2.0 * given[place] - square(tiles, *place, chosen=NEAR[second])
            held = partner if (place[0] == 0) == second else own
            line = SLOTS * order + place[1] - place[0]
            marks[index : index + 1] = held[line : line + 1]

    by_place(compute)


def first_kernel(own, partner, base, marks, norm, two, one, out, pay):
    order = own.shape[-1]

    def compute(second):
        given = pair_tiles(own, partner, second) if second else {}
        far = ((2, 2), (2, 3), (3, 3)) if second else ((-1, 0), (-1, 1), (-2, 0))
        given.update(zip(far, (two[0], two[1], one[...])))
        used = (*far, (0, 2), (1, 2), (1, 3)) if second else far
        tiles = {place: split(given[place]) for place in used}
        after = {}
        for index, place in enumerate(FRONT if second else BACK):
            rest = square(tiles, *place, chosen=FAR[second])
            after[place] = (base[index] - rest) * marks[index : index + 1]
            out[index] = after[place]
        lane = lax.broadcasted_iota(jnp.int32, pay.shape, 1)
        pay[...] = jnp.where(lane == 0, norm[:1], squared_norm(after)) / order

    by_place(compute)


def sides(second):
    here, there = (FRONT, BACK) if second else (BACK, FRONT)
    away = [(row + 2, column + 2) if second else (row - 2, column - 2) for row, column in there]
    return here, there, away


def held_tiles(*groups):
    return {place: split(held[index]) for places, held in groups for index, place in enumerate(places)}


def middle_kernel(own, partner, base):
    def compute(second):
        here, there, _ = sides(second)
        tiles = held_tiles((here, own), (there, partner))
        for index, place in enumerate(here):
            base[index] = square(tiles, *place, chosen=NEAR[second])

    by_place(compute)


def second_kernel(own, partner, base, far, marks, kept, sent):
    def compute(second):
        here, there, away = sides(second)
        tiles = held_tiles((here, own), (away, far)) if second else held_tiles((away, far))
        targets = [sent, kept.at[0], kept.at[1]] if second else [kept.at[0], kept.at[1], sent]
        for index, place in enumerate(here):
            total = base[index] + square(tiles, *place, chosen=FAR[second])
            targets[index][...] = total * marks[index : index + 1]

    by_place(compute)


def cost(products, order):
    return pl.CostEstimate(flops=products * 6 * order**3, bytes_accessed=48 * order**2, transcendentals=0)


def first_step(own, partner, two, one):
    order = own.shape[-1]
    tiles = jax.ShapeDtypeStruct((SLOTS, order, order), jnp.float32)
    lines = jax.ShapeDtypeStruct((MARKS, LANES), jnp.float32)
    norm = pl.pallas_call(
        norm_kernel,
        out_shape=lines,
        in_specs=[VMEM],
        out_specs=VMEM,
        compiler_params=pltpu.CompilerParams(vmem_limit_bytes=2 * MIB),
        cost_estimate=pl.CostEstimate(flops=SPREAD_COST, bytes_accessed=0, transcendentals=0),
    )(own)
    near = pl.pallas_call(
        near_kernel,
        out_shape=[tiles, jax.ShapeDtypeStruct((MARKS, order), jnp.float32)],
        in_specs=[VMEM] * 3,
        out_specs=[VMEM] * 2,
        compiler_params=pltpu.CompilerParams(vmem_limit_bytes=12 * MIB),
        cost_estimate=cost(9, order),
    )(own, partner, norm)
    fresh, pay = pl.pallas_call(
        first_kernel,
        out_shape=[tiles, jax.ShapeDtypeStruct((lax.axis_size(OUTER), LANES), jnp.float32)],
        in_specs=[VMEM] * 7,
        out_specs=[VMEM] * 2,
        compiler_params=pltpu.CompilerParams(vmem_limit_bytes=12 * MIB),
        cost_estimate=cost(5, order),
    )(own, partner, *near, norm, two, one)
    return fresh, near[1], pay


def second_step(own, partner, far, marks):
    order = own.shape[-1]
    base = pl.pallas_call(
        middle_kernel,
        out_shape=jax.ShapeDtypeStruct(own.shape, jnp.float32),
        in_specs=[VMEM] * 2,
        out_specs=VMEM,
        compiler_params=pltpu.CompilerParams(vmem_limit_bytes=12 * MIB),
        cost_estimate=cost(9, order),
    )(own, partner)
    return pl.pallas_call(
        second_kernel,
        out_shape=[
            jax.ShapeDtypeStruct((2, order, order), jnp.float32),
            jax.ShapeDtypeStruct((order, order), jnp.float32),
        ],
        in_specs=[VMEM] * 5,
        out_specs=[VMEM] * 2,
        compiler_params=pltpu.CompilerParams(vmem_limit_bytes=12 * MIB),
        cost_estimate=cost(5, order),
    )(own, partner, base, far, marks)


def join_kernel(kept, received, out, sent):
    second = lax.axis_index("core")
    copies = [
        pltpu.make_async_copy(kept, out.at[pl.ds(second, 2)], sent.at[0]),
        pltpu.make_async_copy(received, out.at[SPAN - SPAN * second], sent.at[1]),
    ]
    for copy in copies:
        copy.start()
    for copy in copies:
        copy.wait()


def join(kept, received):
    order = kept.shape[-1]
    return pl.pallas_call(
        join_kernel,
        out_shape=jax.ShapeDtypeStruct((SLOTS, order, order), jnp.float32),
        in_specs=[VMEM] * 2,
        out_specs=pl.BlockSpec(memory_space=pl.ANY),
        scratch_shapes=[pltpu.SemaphoreType.DMA((2,))],
        compiler_params=pltpu.CompilerParams(vmem_limit_bytes=2 * MIB),
        cost_estimate=pl.CostEstimate(flops=0, bytes_accessed=24 * order**2, transcendentals=0),
    )(kept, received)


def spread_kernel(parts, out):
    total = jnp.sum(parts[...], axis=0, keepdims=True)
    out[...] = jnp.broadcast_to(total, out.shape)


def total_kernel(parts, out):
    out[...] = jnp.sum(parts[...], axis=0, keepdims=True)[:, :STEPS]


def total_of(parts):
    return pl.pallas_call(
        total_kernel,
        out_shape=jax.ShapeDtypeStruct((1, STEPS), jnp.float32),
        in_specs=[VMEM],
        out_specs=VMEM,
        compiler_params=pltpu.CompilerParams(vmem_limit_bytes=MIB),
        cost_estimate=pl.CostEstimate(flops=SPREAD_COST, bytes_accessed=0, transcendentals=0),
    )(parts)


def spread(parts, rows):
    return pl.pallas_call(
        spread_kernel,
        out_shape=jax.ShapeDtypeStruct((rows, LANES), jnp.float32),
        in_specs=[VMEM],
        out_specs=VMEM,
        compiler_params=pltpu.CompilerParams(vmem_limit_bytes=MIB),
        cost_estimate=pl.CostEstimate(flops=SPREAD_COST, bytes_accessed=0, transcendentals=0),
    )(parts)


def body(upper_tiles, listed_mask):
    own, two, one = masked(listed_mask, upper_tiles)
    two, one, partner = (permute(two, -1, 1), permute(one, 2, -2), permute(own, 1, -1))
    fresh, marks, pay = first_step(own, partner, two, one)
    part = spread(lax.all_to_all(pay, OUTER, 0, 0, tiled=True), lax.axis_size(INNER))
    part, marks = lax.optimization_barrier((part, marks))
    kept, sent = second_step(fresh, permute(fresh, 1, -1), permute(fresh, -1, 1), marks)
    gathered = lax.all_to_all(part, INNER, 0, 0, tiled=True)
    total = total_of(gathered)
    kept, total = lax.optimization_barrier((kept, total))
    purified = join(kept, permute(sent, 1, -1))
    traces = total[0]
    return (purified[None], traces)


def solution(mesh):
    rows, columns = mesh.devices.shape
    parted = Mesh(mesh.devices.reshape(rows // 4, 4, columns // 2, 2), AXES)
    return jax.shard_map(
        body,
        mesh=parted,
        in_specs=(P(AXES), P(AXES)),
        out_specs=(P(AXES), P()),
        check_vma=False,
    )
```

```python
import jax
import jax.numpy as jnp
from jax import lax
from jax.experimental import pallas as pl
from jax.experimental.pallas import tpu as pltpu
from jax.sharding import Mesh
from jax.sharding import PartitionSpec as P

STEPS = 2
SLOTS = 3
SPAN = SLOTS - 1
AXES = ("z", "x", "y", "core")
INNER = ("z", "core")
OUTER = ("x", "y")
LANES = 128
MARKS = 8
MIB = 1024 * 1024
SPREAD_COST = 10**11

VMEM = pl.BlockSpec(memory_space=pltpu.VMEM)

BACK = ((0, 0), (0, 1), (1, 1))
FRONT = ((0, 2), (1, 2), (1, 3))
NEAR = ((0, 1, 2, 3), (0, 1))
FAR = ((-2, -1), (2, 3))


def permute(value, first_shift, second_shift):
    count = lax.axis_size(AXES)
    moves = [(source, source + (second_shift if source % 2 else first_shift)) for source in range(count)]
    return lax.ppermute(value, AXES, [move for move in moves if 0 <= move[1] < count])


def split(tile):
    high = tile.astype(jnp.bfloat16)
    return (high, (tile - high.astype(jnp.float32)).astype(jnp.bfloat16))


def product(left, right, left_dim, right_dim):
    def one(a, b):
        return lax.dot_general(
            a, b, (((left_dim,), (right_dim,)), ((), ())), preferred_element_type=jnp.float32
        )

    return one(left[0], right[0]) + (one(left[0], right[1]) + one(left[1], right[0]))


def square(tiles, row, column, chosen=None):
    total = None
    for middle in range(max(row, column) - SPAN, min(row, column) + SPAN + 1):
        if chosen is not None and middle not in chosen:
            continue
        left = tiles[min(row, middle), max(row, middle)]
        right = tiles[min(middle, column), max(middle, column)]
        term = product(left, right, 1 if row <= middle else 0, 0 if middle <= column else 1)
        total = term if total is None else total + term
    return total


def squared_norm(tiles):
    total = 0.0
    for (row, column), tile in tiles.items():
        total = total + (1.0 if row == column else 2.0) * jnp.sum(tile * tile)
    return total


def by_place(kernel):
    second = lax.axis_index("core")
    for place in range(2):

        @pl.when(second == place)
        def _():
            kernel(place == 1)


def mask_kernel(rows_total, mask, upper, own, two, one, held, buffer, arrived):
    order = upper.shape[-1]
    flags = pltpu.make_async_copy(mask, held, arrived.at[SLOTS])
    flags.start()
    copies = [
        pltpu.make_async_copy(upper.at[0, slot], buffer.at[slot], arrived.at[slot]) for slot in range(SLOTS)
    ]
    for copy in copies:
        copy.start()
    here = lax.axis_index(AXES)
    second = lax.axis_index("core")
    line = lax.broadcasted_iota(jnp.int32, (MARKS, order), 0)
    marks = jnp.zeros((MARKS, order), jnp.float32)
    flags.wait()
    weights = [
        jnp.where(here + slot < rows_total, held[0, slot], 0).astype(jnp.float32) for slot in range(SLOTS)
    ]
    for slot in range(SLOTS):
        marks = jnp.where(line == slot, weights[slot], marks)
    own[SLOTS * order :] = marks
    for slot in range(SLOTS):
        copies[slot].wait()
        tile = buffer[slot] * weights[slot]
        own[slot * order : (slot + 1) * order] = tile
        for place in range(2):

            @pl.when(second == place)
            def _():
                if 0 <= slot - place < 2:
                    two[slot - place] = tile
                else:
                    one[...] = tile


def masked(mask, upper):
    order = upper.shape[-1]
    rows_total = lax.axis_size(AXES)
    return pl.pallas_call(
        lambda *refs: mask_kernel(rows_total, *refs),
        out_shape=[
            jax.ShapeDtypeStruct((SLOTS * order + MARKS, order), jnp.float32),
            jax.ShapeDtypeStruct((2, order, order), jnp.float32),
            jax.ShapeDtypeStruct((order, order), jnp.float32),
        ],
        in_specs=[pl.BlockSpec(memory_space=pl.ANY)] * 2,
        out_specs=[VMEM] * 3,
        scratch_shapes=[
            pltpu.SMEM(mask.shape, jnp.int32),
            pltpu.VMEM((SLOTS, order, order), jnp.float32),
            pltpu.SemaphoreType.DMA((SLOTS + 1,)),
        ],
        compiler_params=pltpu.CompilerParams(vmem_limit_bytes=8 * MIB),
        cost_estimate=pl.CostEstimate(flops=0, bytes_accessed=36 * order**2, transcendentals=0),
    )(pltpu.with_memory_space_constraint(mask, pltpu.HBM), pltpu.with_memory_space_constraint(upper, pltpu.HBM))


def pair_tiles(own, partner, second):
    order = own.shape[-1]
    return {
        (row, row + slot): held[slot * order : (slot + 1) * order]
        for row, held in enumerate((partner, own) if second else (own, partner))
        for slot in range(SLOTS)
    }


def norm_kernel(own, norm):
    order = own.shape[-1]
    tiles = {(0, slot): own[slot * order : (slot + 1) * order] for slot in range(SLOTS)}
    norm[...] = jnp.full(norm.shape, squared_norm(tiles), jnp.float32)


def near_kernel(own, partner, norm, base, marks):
    order = own.shape[-1]

    def compute(second):
        given = pair_tiles(own, partner, second)
        tiles = {place: split(tile) for place, tile in given.items()}
        for index, place in enumerate(FRONT if second else BACK):
            base[index] = 2.0 * given[place] - square(tiles, *place, chosen=NEAR[second])
            held = partner if (place[0] == 0) == second else own
            line = SLOTS * order + place[1] - place[0]
            marks[index : index + 1] = held[line : line + 1]

    by_place(compute)


def first_kernel(own, partner, base, marks, norm, two, one, out, pay):
    order = own.shape[-1]

    def compute(second):
        given = pair_tiles(own, partner, second) if second else {}
        far = ((2, 2), (2, 3), (3, 3)) if second else ((-1, 0), (-1, 1), (-2, 0))
        given.update(zip(far, (two[0], two[1], one[...])))
        used = (*far, (0, 2), (1, 2), (1, 3)) if second else far
        tiles = {place: split(given[place]) for place in used}
        after = {}
        for index, place in enumerate(FRONT if second else BACK):
            rest = square(tiles, *place, chosen=FAR[second])
            after[place] = (base[index] - rest) * marks[index : index + 1]
            out[index] = after[place]
        lane = lax.broadcasted_iota(jnp.int32, pay.shape, 1)
        pay[...] = jnp.where(lane == 0, norm[:1], squared_norm(after)) / order

    by_place(compute)


def sides(second):
    here, there = (FRONT, BACK) if second else (BACK, FRONT)
    away = [(row + 2, column + 2) if second else (row - 2, column - 2) for row, column in there]
    return here, there, away


def held_tiles(*groups):
    return {place: split(held[index]) for places, held in groups for index, place in enumerate(places)}


def middle_kernel(own, partner, base):
    def compute(second):
        here, there, _ = sides(second)
        tiles = held_tiles((here, own), (there, partner))
        for index, place in enumerate(here):
            base[index] = square(tiles, *place, chosen=NEAR[second])

    by_place(compute)


def second_kernel(own, partner, base, far, marks, kept, sent):
    def compute(second):
        here, there, away = sides(second)
        tiles = held_tiles((here, own), (away, far)) if second else held_tiles((away, far))
        targets = [sent, kept.at[0], kept.at[1]] if second else [kept.at[0], kept.at[1], sent]
        for index, place in enumerate(here):
            total = base[index] + square(tiles, *place, chosen=FAR[second])
            targets[index][...] = total * marks[index : index + 1]

    by_place(compute)


def cost(products, order):
    return pl.CostEstimate(flops=products * 6 * order**3, bytes_accessed=48 * order**2, transcendentals=0)


def first_step(own, partner, two, one):
    order = own.shape[-1]
    tiles = jax.ShapeDtypeStruct((SLOTS, order, order), jnp.float32)
    lines = jax.ShapeDtypeStruct((MARKS, LANES), jnp.float32)
    norm = pl.pallas_call(
        norm_kernel,
        out_shape=lines,
        in_specs=[VMEM],
        out_specs=VMEM,
        compiler_params=pltpu.CompilerParams(vmem_limit_bytes=2 * MIB),
        cost_estimate=pl.CostEstimate(flops=SPREAD_COST, bytes_accessed=0, transcendentals=0),
    )(own)
    near = pl.pallas_call(
        near_kernel,
        out_shape=[tiles, jax.ShapeDtypeStruct((MARKS, order), jnp.float32)],
        in_specs=[VMEM] * 3,
        out_specs=[VMEM] * 2,
        compiler_params=pltpu.CompilerParams(vmem_limit_bytes=12 * MIB),
        cost_estimate=cost(9, order),
    )(own, partner, norm)
    fresh, pay = pl.pallas_call(
        first_kernel,
        out_shape=[tiles, jax.ShapeDtypeStruct((lax.axis_size(OUTER), LANES), jnp.float32)],
        in_specs=[VMEM] * 7,
        out_specs=[VMEM] * 2,
        compiler_params=pltpu.CompilerParams(vmem_limit_bytes=12 * MIB),
        cost_estimate=cost(5, order),
    )(own, partner, *near, norm, two, one)
    return fresh, near[1], pay


def second_step(own, partner, far, marks):
    order = own.shape[-1]
    base = pl.pallas_call(
        middle_kernel,
        out_shape=jax.ShapeDtypeStruct(own.shape, jnp.float32),
        in_specs=[VMEM] * 2,
        out_specs=VMEM,
        compiler_params=pltpu.CompilerParams(vmem_limit_bytes=12 * MIB),
        cost_estimate=cost(9, order),
    )(own, partner)
    return pl.pallas_call(
        second_kernel,
        out_shape=[
            jax.ShapeDtypeStruct((2, order, order), jnp.float32),
            jax.ShapeDtypeStruct((order, order), jnp.float32),
        ],
        in_specs=[VMEM] * 5,
        out_specs=[VMEM] * 2,
        compiler_params=pltpu.CompilerParams(vmem_limit_bytes=12 * MIB),
        cost_estimate=cost(5, order),
    )(own, partner, base, far, marks)


def join_kernel(kept, received, out, sent):
    second = lax.axis_index("core")
    copies = [
        pltpu.make_async_copy(kept, out.at[pl.ds(second, 2)], sent.at[0]),
        pltpu.make_async_copy(received, out.at[SPAN - SPAN * second], sent.at[1]),
    ]
    for copy in copies:
        copy.start()
    for copy in copies:
        copy.wait()


def join(kept, received):
    order = kept.shape[-1]
    return pl.pallas_call(
        join_kernel,
        out_shape=jax.ShapeDtypeStruct((SLOTS, order, order), jnp.float32),
        in_specs=[VMEM] * 2,
        out_specs=pl.BlockSpec(memory_space=pl.ANY),
        scratch_shapes=[pltpu.SemaphoreType.DMA((2,))],
        compiler_params=pltpu.CompilerParams(vmem_limit_bytes=2 * MIB),
        cost_estimate=pl.CostEstimate(flops=0, bytes_accessed=24 * order**2, transcendentals=0),
    )(kept, received)


def spread_kernel(parts, out):
    total = jnp.sum(parts[...], axis=0, keepdims=True)
    out[...] = jnp.broadcast_to(total, out.shape)


def total_kernel(parts, out):
    out[...] = jnp.sum(parts[...], axis=0, keepdims=True)[:, :STEPS]


def total_of(parts):
    return pl.pallas_call(
        total_kernel,
        out_shape=jax.ShapeDtypeStruct((1, STEPS), jnp.float32),
        in_specs=[VMEM],
        out_specs=VMEM,
        compiler_params=pltpu.CompilerParams(vmem_limit_bytes=MIB),
        cost_estimate=pl.CostEstimate(flops=SPREAD_COST, bytes_accessed=0, transcendentals=0),
    )(parts)


def spread(parts, rows):
    return pl.pallas_call(
        spread_kernel,
        out_shape=jax.ShapeDtypeStruct((rows, LANES), jnp.float32),
        in_specs=[VMEM],
        out_specs=VMEM,
        compiler_params=pltpu.CompilerParams(vmem_limit_bytes=MIB),
        cost_estimate=pl.CostEstimate(flops=SPREAD_COST, bytes_accessed=0, transcendentals=0),
    )(parts)


def body(upper_tiles, listed_mask):
    own, two, one = masked(listed_mask, upper_tiles)
    two, one, partner = (permute(two, -1, 1), permute(one, 2, -2), permute(own, 1, -1))
    fresh, marks, pay = first_step(own, partner, two, one)
    part = spread(lax.all_to_all(pay, OUTER, 0, 0, tiled=True), lax.axis_size(INNER))
    part, marks = lax.optimization_barrier((part, marks))
    kept, sent = second_step(fresh, permute(fresh, 1, -1), permute(fresh, -1, 1), marks)
    gathered = lax.all_to_all(part, INNER, 0, 0, tiled=True)
    total = total_of(gathered)
    kept, total = lax.optimization_barrier((kept, total))
    purified = join(kept, permute(sent, 1, -1))
    traces = total[0]
    return (purified[None], traces)


def solution(mesh):
    rows, columns = mesh.devices.shape
    parted = Mesh(mesh.devices.reshape(rows // 4, 4, columns // 2, 2), AXES)
    return jax.shard_map(
        body,
        mesh=parted,
        in_specs=(P(AXES), P(AXES)),
        out_specs=(P(AXES), P()),
        check_vma=False,
    )
```
